32 devices in a mesh: row: 4 (over y, x), col: 8 (over z, core).
Axes of the slice: x: 2, y: 2, z: 4, core: 2. Of those that a mesh axis runs over, the one named last changes fastest.
Arguments:
- vectors: bfloat16 [64, 131072], P(None, ('col', 'row')), may hold values from -6 to 6
- blocks: bfloat16 [4, 4096, 128, 128], P('row', 'col'), may hold values from -0.1875 to 0.1875
- block_rows: int32 [4, 4096], P('row', 'col'), may hold values from 0 to 255, as said below
- block_cols: int32 [4, 4096], P('row', 'col'), may hold values from 0 to 127, as said below
- counts: int32 [4, 8], P('row', 'col'), may hold values from 1 to 512, as said below
Outputs:
- result: float32 [64, 131072], P(None, ('row', 'col'))
The draws below stay inside these ranges and needn't reach their ends.
Inputs may be any that keep to these rules, and one draw needn't show every extreme that they name: Within one owner pair the slots below its count name distinct positions (block_rows, block_cols) of its 256 x 256/2 grid of blocks; later slots hold 0. `block_cols`: see block_rows. `counts`: some owner pair holds exactly 512 blocks, and some other exactly one.
All inputs are finite; a program needn't handle non-finite values.
Results may differ from the reference program's by a relative error of at most 0.0029.
Values may be sent and summed in bfloat16 or wider, within the bound.
No kernel may reach another device: no remote copies, remote signals or barrier semaphores. Data moves between devices by JAX's collectives and lax.ppermute only.
A program may use at most 128 MiB of HBM per device.

```python
import jax
import jax.numpy as jnp
from jax import lax

BS = 128
K = 64
RB = 256
CAP = 512
N = 131072
N_ROW = 4
N_COL = 8


def block_pattern(key):
    devices = N_ROW * N_COL
    grid_cells = RB * (RB // 2)
    base_key = jax.random.fold_in(key, 7)
    key_perm, key_base, key_level, key_full, key_least = jax.random.split(base_key, 5)
    owner_keys = jax.random.split(key_perm, devices)
    positions = jax.vmap(lambda subkey: jax.random.permutation(subkey, grid_cells))(owner_keys)[:, :CAP]
    base_count = jax.random.randint(key_base, (N_ROW, N_COL), CAP // 8, CAP // 4 + 1)
    row_level = jax.random.randint(key_level, (N_ROW, 1), 0, 4)
    row_factor = jnp.where(row_level == 3, 4, jnp.where(row_level == 2, 2, 1))
    slot_counts = jnp.minimum(base_count * row_factor, CAP)
    fullest = jax.random.randint(key_full, (), 0, devices)
    least = (fullest + 1 + jax.random.randint(key_least, (), 0, devices - 1)) % devices
    owner_ids = jnp.arange(devices, dtype=jnp.int32).reshape(N_ROW, N_COL)
    slot_counts = jnp.where(owner_ids == fullest, CAP, slot_counts)
    slot_counts = jnp.where(owner_ids == least, 1, slot_counts).astype(jnp.int32)
    live_slots = jnp.arange(CAP, dtype=jnp.int32)[None, :] < slot_counts.reshape(devices, 1)
    positions = jnp.where(live_slots, positions, 0).astype(jnp.int32)
    row_ids = (positions // (RB // 2)).reshape(N_ROW, N_COL * CAP).astype(jnp.int32)
    col_ids = (positions % (RB // 2)).reshape(N_ROW, N_COL * CAP).astype(jnp.int32)
    return (row_ids, col_ids, slot_counts)


def draw_block_rows(key, part):
    return block_pattern(key)[0]


def draw_block_cols(key, part):
    return block_pattern(key)[1]


def draw_counts(key, part):
    return block_pattern(key)[2]


def steps_of(key, dims, cuts, low, high):
    factor_of = 1.0
    for axis_at, blocks in cuts:
        draws = jax.random.uniform(jax.random.fold_in(jax.random.fold_in(key, 6), axis_at), (blocks,), jnp.float32, low / len(cuts), high / len(cuts))
        factor_of = factor_of * jnp.repeat(jnp.exp(draws), dims[axis_at] // blocks).reshape((-1,) + (1,) * (len(dims) - 1 - axis_at))
    return factor_of


def scatter_about(rng, dims, deviation, limit, shards=(), kind=jnp.bfloat16):
    array = jax.random.normal(rng, dims, jnp.float32) * deviation
    if len(shards) > 0:
        array = steps_of(rng, dims, shards, -0.22, 0.18) * array
    return jnp.clip(array, min=-limit, max=limit).astype(kind)


def setup_inputs(seed: int = 0) -> dict:
    seeds = jax.random.split(jax.random.key(seed), 6)
    vectors = scatter_about(seeds[0], (K, N), 1.0, 6.0, ((1, 32),))
    blocks = scatter_about(seeds[1], (N_ROW, N_COL * CAP, BS, BS), (BS * CAP * N_COL // (2 * RB)) ** -0.5, 0.1875, ((0, 4), (1, 8)))
    block_rows = draw_block_rows(jax.random.fold_in(seeds[5], 71), 0)
    block_cols = draw_block_cols(jax.random.fold_in(seeds[5], 71), 0)
    counts = draw_counts(jax.random.fold_in(seeds[5], 71), 0)
    return {"vectors": vectors, "blocks": blocks, "block_rows": block_rows, "block_cols": block_cols, "counts": counts}


def owner_part(vec_panel, owner_blocks, row_ids, col_ids, slot_count):
    vec_width = vec_panel.shape[0]
    vec_tiles = vec_panel.reshape(vec_width, RB // 2, BS)
    picked = jnp.take(vec_tiles, col_ids, axis=1).astype(jnp.float32)
    product = jnp.einsum("ksc,src->ksr", picked, owner_blocks.astype(jnp.float32), precision=lax.Precision.HIGHEST)
    live_slots = (jnp.arange(CAP, dtype=jnp.int32) < slot_count).astype(jnp.float32)
    product = product * live_slots[None, :, None]
    summed = jax.ops.segment_sum(jnp.moveaxis(product, 1, 0), row_ids, num_segments=RB)
    return jnp.moveaxis(summed, 0, 1).reshape(vec_width, RB * BS)


def apply_matrix(vectors, blocks, block_rows, block_cols, counts):
    group_width = RB * BS // 2
    all_blocks = blocks.reshape(N_ROW * N_COL, CAP, BS, BS)
    all_rows = block_rows.reshape(N_ROW * N_COL, CAP)
    all_cols = block_cols.reshape(N_ROW * N_COL, CAP)
    all_counts = counts.reshape(N_ROW * N_COL)

    def add_owner(running, owner):
        row_owner = owner // N_COL
        col_owner = owner % N_COL
        vec_panel = lax.dynamic_slice_in_dim(vectors, col_owner * group_width, group_width, 1)
        part = owner_part(vec_panel, all_blocks[owner], all_rows[owner], all_cols[owner], all_counts[owner])
        current = lax.dynamic_slice_in_dim(running, row_owner * (RB * BS), RB * BS, 1)
        return lax.dynamic_update_slice_in_dim(running, current + part, row_owner * (RB * BS), 1), None

    running = jnp.zeros((K, N), jnp.float32)
    running, _ = lax.scan(add_owner, running, jnp.arange(N_ROW * N_COL, dtype=jnp.int32))
    return running


def reference(vectors, blocks, block_rows, block_cols, counts):
    first = apply_matrix(vectors, blocks, block_rows, block_cols, counts).astype(jnp.bfloat16)
    return apply_matrix(first, blocks, block_rows, block_cols, counts)
```

```python
import functools

import jax
import jax.numpy as jnp
import numpy as np
from jax import lax
from jax.experimental import pallas as pl
from jax.experimental.pallas import tpu as pltpu
from jax.sharding import PartitionSpec as P

GROUP = 8
CHUNK = 32
UNROLL = 4
TOP = 14.0
VMEM_LIMIT = 60 * 1024 * 1024


def message_rows(vec_width):
    return GROUP * vec_width + 16


def encode(tiles, ref):
    k = tiles[0].shape[0]
    exponents = []
    for i, tile in enumerate(tiles):
        peak = jnp.max(jnp.abs(tile), axis=0, keepdims=True)
        exponent = jnp.ceil(jnp.log2(jnp.maximum(peak, 1e-30)))
        scaled = jnp.round(tile * jnp.exp2(TOP - exponent))
        ref[i * k : (i + 1) * k, :] = scaled.astype(jnp.int32).astype(jnp.int16)
        exponents.append(exponent)
    rest = jnp.zeros((16 - len(tiles), tiles[0].shape[1]), jnp.float32)
    table = jnp.concatenate(exponents + [rest], axis=0)
    ref[len(tiles) * k :, :] = table.astype(jnp.int32).astype(jnp.int16)


def decoder(ref, k, factor=None):
    table = ref[GROUP * k :, :].astype(jnp.int32).astype(jnp.float32)
    scale = jnp.exp2(table - TOP)
    if factor is not None:
        scale = scale * factor

    def tile(i):
        codes = ref[i * k : (i + 1) * k, :].astype(jnp.int32).astype(jnp.float32)
        return codes * scale[i : i + 1, :]

    return tile


def product_kernel(places, row_axis, shard, rows, cols, count, *refs):
    pieces = refs[: len(places)]
    blocks, own, msg, panel, held, acc, out, piece_sem, block_sem, own_sem, msg_sem = refs[len(places) :]
    chips = own.shape[0]
    row_total = acc.shape[0] - 1
    slots = blocks.shape[0]
    n = count[0, 0]
    core = lax.axis_index("col") % 2
    row_owner = lax.axis_index(row_axis)

    def piece_copy(i):
        flip, offset = places[i]
        at = (row_owner ^ flip) * shard + offset if flip is not None else offset
        return pltpu.make_async_copy(
            pieces[i], panel.at[pl.ds(at, pieces[i].shape[0])], piece_sem.at[i]
        )

    def block_copy(i):
        span = pl.ds(i * CHUNK, CHUNK)
        return pltpu.make_async_copy(blocks.at[span], held.at[span], block_sem.at[i])

    for i in range(len(places)):
        piece_copy(i).start()
    for i in range(slots // CHUNK):

        @pl.when(i * CHUNK < n)
        def _():
            block_copy(i).start()

    @pl.loop(0, row_total + 1)
    def _(i):
        acc[i] = jnp.zeros_like(acc[0])

    for i in range(len(places)):
        piece_copy(i).wait()

    @pl.loop(0, (n + CHUNK - 1) // CHUNK)
    def _(c):
        block_copy(c).wait()
        first = c * CHUNK
        groups = (jnp.minimum(n - first, CHUNK) + UNROLL - 1) // UNROLL

        @pl.loop(0, groups)
        def _(g):
            base = first + g * UNROLL
            products = []
            for u in range(UNROLL):
                products.append(
                    lax.dot_general(
                        panel[cols[0, base + u]],
                        held[base + u],
                        (((1,), (1,)), ((), ())),
                        preferred_element_type=jnp.float32,
                    )
                )
            for u in range(UNROLL):
                at = jnp.where(base + u < n, rows[0, base + u], row_total)
                acc[at] += products[u]

    def own_copy(d):
        return pltpu.make_async_copy(
            acc.at[pl.ds((2 * d + core) * shard, shard)], own.at[d], own_sem.at[d]
        )

    def msg_copy(d):
        return pltpu.make_async_copy(out.at[d], msg.at[d], msg_sem.at[d])

    for d in range(chips):
        own_copy(d).start()
    for d in range(chips):
        base = (2 * d + 1 - core) * shard

        @pl.loop(0, shard // GROUP)
        def _(g):
            tiles = [acc[base + g * GROUP + i] for i in range(GROUP)]
            encode(tiles, out.at[d, g])

        msg_copy(d).start()
    for d in range(chips):
        own_copy(d).wait()
        msg_copy(d).wait()


def block_product(pieces, places, blocks, block_rows, block_cols, counts, shard, col_total):
    slots, order, _ = blocks.shape
    k = pieces[0].shape[1]
    chips = col_total // 2
    panel_tiles = sum(p.shape[0] for p in pieces)
    groups = shard // GROUP
    scalars = pl.BlockSpec(memory_space=pltpu.SMEM)
    anywhere = pl.BlockSpec(memory_space=pl.ANY)
    return pl.pallas_call(
        functools.partial(product_kernel, places, "row", shard),
        out_shape=(
            jax.ShapeDtypeStruct((chips, shard, k, order), jnp.float32),
            jax.ShapeDtypeStruct((chips, groups, message_rows(k), order), jnp.int16),
        ),
        in_specs=[scalars] * 3 + [anywhere] * (len(pieces) + 1),
        out_specs=(anywhere, anywhere),
        scratch_shapes=[
            pltpu.VMEM((panel_tiles, k, order), jnp.bfloat16),
            pltpu.VMEM((slots, order, order), jnp.bfloat16),
            pltpu.VMEM((col_total * shard + 1, k, order), jnp.float32),
            pltpu.VMEM((chips, groups, message_rows(k), order), jnp.int16),
            pltpu.SemaphoreType.DMA((len(pieces),)),
            pltpu.SemaphoreType.DMA((slots // CHUNK,)),
            pltpu.SemaphoreType.DMA((chips,)),
            pltpu.SemaphoreType.DMA((chips,)),
        ],
        compiler_params=pltpu.CompilerParams(vmem_limit_bytes=VMEM_LIMIT),
        name="block_product",
    )(block_rows, block_cols, counts, *pieces, blocks)


def combine_kernel(which, flags, form, meta, own, sib, *refs):
    arrived, result = refs[:-1], refs[-1]
    k = own.shape[2]
    parts = [decoder(sib.at[0, 0], k)]
    for ref, flag in zip(arrived, flags):
        factor = None if flag is None else meta[flag].astype(jnp.float32)
        parts.append(decoder(ref.at[0], k, factor))

    def total(i):
        tile = own[0, i]
        for part in parts:
            tile = tile + part(i)
        return tile

    if form == "message":
        encode([total(i) for i in range(GROUP)], result.at[0])
    elif form == "tiles":
        for i in range(GROUP):
            result[i] = total(i).astype(result.dtype)
    else:
        order = own.shape[3]
        for i in range(GROUP):
            result[:, i * order : (i + 1) * order] = total(i)


def combine(meta, which, own, sib, arrived, flags, form):
    _, shard, k, order = own.shape
    groups = shard // GROUP
    rows = message_rows(k)
    message = pl.BlockSpec((1, rows, order), lambda g, meta: (g, 0, 0))
    if form == "message":
        out_shape, out_spec = jax.ShapeDtypeStruct((groups, rows, order), jnp.int16), message
    elif form == "tiles":
        out_shape = jax.ShapeDtypeStruct((shard, k, order), jnp.bfloat16)
        out_spec = pl.BlockSpec((GROUP, k, order), lambda g, meta: (g, 0, 0))
    else:
        out_shape = jax.ShapeDtypeStruct((k, shard * order), jnp.float32)
        out_spec = pl.BlockSpec((k, GROUP * order), lambda g, meta: (0, g))
    return pl.pallas_call(
        functools.partial(combine_kernel, which, flags, form),
        out_shape=out_shape,
        grid_spec=pltpu.PrefetchScalarGridSpec(
            num_scalar_prefetch=1,
            grid=(groups,),
            in_specs=[
                pl.BlockSpec((1, GROUP, k, order), lambda g, meta: (meta[which], g, 0, 0)),
                pl.BlockSpec((1, 1, rows, order), lambda g, meta: (meta[which], g, 0, 0)),
            ]
            + [message] * len(arrived),
            out_specs=out_spec,
        ),
        name="combine_" + form,
    )(meta, own, sib, *arrived)


def chip_moves(chips, cores, moves):
    return [(cores * a + c, cores * b + c) for a, b in moves for c in range(cores)]


LINE = np.array([[3, 2, 1, 0, 0, 1], [0, 3, 2, 1, 1, 0], [3, 0, 1, 2, 1, 0], [0, 1, 2, 3, 0, 1]], np.int32)


def sum_over_col(own, msg, form):
    col_total = 2 * own.shape[0]
    chips = own.shape[0]
    place = lax.axis_index("col") // 2
    pair = [(c, c ^ 1) for c in range(col_total)]
    if chips == 4:
        meta = jnp.asarray(LINE)[place]
        sib = lax.ppermute(msg, "col", pair)
        send = combine(meta, 0, own, sib, (), (), "message")
        got_a = lax.ppermute(send, "col", chip_moves(chips, 2, [(0, 1), (1, 0), (2, 3), (3, 2)]))
        send = combine(meta, 1, own, sib, (got_a,), (4,), "message")
        got_b = lax.ppermute(send, "col", chip_moves(chips, 2, [(0, 1), (3, 2), (1, 3), (2, 0)]))
        send = combine(meta, 2, own, sib, (got_b,), (4,), "message")
        got_c = lax.ppermute(send, "col", chip_moves(chips, 2, [(0, 1), (3, 2)]))
        got_d = lax.ppermute(send, "col", chip_moves(chips, 2, [(1, 2), (2, 1)]))
        return combine(meta, 3, own, sib, (got_a, got_b, got_c, got_d), (5, 5, None, None), form)
    meta = (place + jnp.arange(chips, dtype=jnp.int32)) % chips
    sib = lax.ppermute(msg, "col", pair)
    arrived = []
    for step in range(1, chips):
        send = combine(meta, step, own, sib, (), (), "message")
        moves = [(a, (a + step) % chips) for a in range(chips)]
        arrived.append(lax.ppermute(send, "col", chip_moves(chips, 2, moves)))
    return combine(meta, 0, own, sib, tuple(arrived), (None,) * len(arrived), form)


def gather_panel(tiles, row_total):
    shard = tiles.shape[0]
    if row_total == 4:
        half = shard // 2
        flip = lambda bit: [(r, r ^ bit) for r in range(4)]
        near_x = lax.ppermute(tiles, "row", flip(1))
        near_y = lax.ppermute(tiles, "row", flip(2))
        far_low = lax.ppermute(near_y[:half], "row", flip(1))
        far_high = lax.ppermute(near_x[half:], "row", flip(2))
        places = ((0, 0), (1, 0), (2, 0), (3, 0), (3, half))
        return (tiles, near_x, near_y, far_low, far_high), places
    return (lax.all_gather(tiles, "row", axis=0, tiled=True),), ((None, 0),)


def shards(row_total, col_total, vectors, blocks, block_rows, block_cols, counts):
    k, width = vectors.shape
    order = blocks.shape[2]
    shard = width // order
    matrix = (blocks[0], block_rows, block_cols, counts, shard, col_total)
    tiles = vectors.reshape(k, shard, order).transpose(1, 0, 2)
    first = sum_over_col(*block_product(*gather_panel(tiles, row_total), *matrix), "tiles")
    moves = []
    for s in range(row_total * col_total):
        moves.append((s, (s % row_total) * col_total + s // row_total))
    tiles = lax.ppermute(first, ("row", "col"), moves)
    return sum_over_col(*block_product(*gather_panel(tiles, row_total), *matrix), "rows")


def solution(mesh):
    in_specs = (
        P(None, ("col", "row")),
        P("row", "col", None, None),
        P("row", "col"),
        P("row", "col"),
        P("row", "col"),
    )
    out_specs = P(None, ("row", "col"))
    body = functools.partial(shards, mesh.shape["row"], mesh.shape["col"])
    return jax.shard_map(body, mesh=mesh, in_specs=in_specs, out_specs=out_specs, check_vma=False)
```

```python
import functools

import jax
import jax.numpy as jnp
from jax import lax
from jax.experimental import pallas as pl
from jax.experimental.pallas import tpu as pltpu
from jax.sharding import PartitionSpec as P

GROUP = 8
STEP = 32
TOP = 14.0
VMEM_LIMIT = 60 * 1024 * 1024

def message_rows(vec_width):
    return GROUP * vec_width + 16


def encode(tiles, ref):
    k = tiles[0].shape[0]
    exponents = []
    for i, tile in enumerate(tiles):
        peak = jnp.max(jnp.abs(tile), axis=0, keepdims=True)
        exponent = jnp.ceil(jnp.log2(jnp.maximum(peak, 1e-30)))
        scaled = jnp.round(tile * jnp.exp2(TOP - exponent))
        ref[i * k : (i + 1) * k, :] = scaled.astype(jnp.int32).astype(jnp.int16)
        exponents.append(exponent)
    rest = jnp.zeros((16 - len(tiles), tiles[0].shape[1]), jnp.float32)
    table = jnp.concatenate(exponents + [rest], axis=0)
    ref[len(tiles) * k :, :] = table.astype(jnp.int32).astype(jnp.int16)


def decoder(ref, k, factor=None):
    table = ref[GROUP * k :, :].astype(jnp.int32).astype(jnp.float32)
    scale = jnp.exp2(table - TOP)
    if factor is not None:
        scale = scale * factor

    def tile(i):
        codes = ref[i * k : (i + 1) * k, :].astype(jnp.int32).astype(jnp.float32)
        return codes * scale[i : i + 1, :]

    return tile


def product_kernel(places, shard, rows, cols, count, *refs):
    total = len(refs) - 12
    pieces = refs[:total]
    blocks, own, msg_low, msg_high, panel, held, acc, out, piece_sem, block_sem, own_sem, msg_sem = refs[total:]
    chips, groups = out.shape[:2]
    k = panel.shape[1]
    row_total = acc.shape[0] - 1
    slots = blocks.shape[0]
    n = count[0, 0]
    core = lax.axis_index("col") % 2
    row_owner = lax.axis_index("row")

    def piece_copy(i):
        piece, start, tiles, at = places[i]
        return pltpu.make_async_copy(
            pieces[piece].at[pl.ds(start, tiles)], panel.at[pl.ds(at(row_owner), tiles)], piece_sem.at[i]
        )

    def block_copy(i):
        span = pl.ds(i * STEP, STEP)
        return pltpu.make_async_copy(blocks.at[span], held.at[span], block_sem.at[i])

    for i in range(len(places)):
        piece_copy(i).start()
    for i in range(slots // STEP):

        @pl.when(i * STEP < n)
        def _():
            block_copy(i).start()

    @pl.loop(0, row_total + 1)
    def _(i):
        acc[i] = jnp.zeros_like(acc[0])

    for i in range(len(places)):
        piece_copy(i).wait()

    @pl.loop(0, (n + STEP - 1) // STEP)
    def _(step):
        block_copy(step).wait()
        base = step * STEP
        nil = jnp.zeros(panel.shape[1:], panel.dtype)
        products = []
        for u in range(0, STEP, 2):
            upper = jnp.concatenate([panel[cols[0, base + u]], nil], axis=1)
            lower = jnp.concatenate([nil, panel[cols[0, base + u + 1]]], axis=1)
            both = lax.dot_general(
                jnp.concatenate([upper, lower], axis=0),
                jnp.concatenate([held[base + u], held[base + u + 1]], axis=1),
                (((1,), (1,)), ((), ())),
                preferred_element_type=jnp.float32,
            )
            products += [both[:k], both[k:]]
        for u in range(STEP):
            at = jnp.where(base + u < n, rows[0, base + u], row_total)
            acc[at] += products[u]

    def own_copy(d):
        return pltpu.make_async_copy(
            acc.at[pl.ds((2 * d + core) * shard, shard)], own.at[d], own_sem.at[d]
        )

    def msg_copy(half, d):
        there = (msg_low, msg_high)[half].at[d]
        return pltpu.make_async_copy(out.at[d, pl.ds(half * (groups // 2), groups // 2)], there, msg_sem.at[half, d])

    for d in range(chips):
        own_copy(d).start()
    for half in range(2):
        for d in range(chips):
            base = (2 * d + 1 - core) * shard

            @pl.loop(half * (groups // 2), (half + 1) * (groups // 2))
            def _(g):
                tiles = [acc[base + g * GROUP + i] for i in range(GROUP)]
                encode(tiles, out.at[d, g])

            msg_copy(half, d).start()
    for d in range(chips):
        own_copy(d).wait()
        msg_copy(0, d).wait()
        msg_copy(1, d).wait()


def block_product(pieces, places, blocks, block_rows, block_cols, counts, shard, col_total):
    slots, order, _ = blocks.shape
    k = pieces[0].shape[1]
    chips = col_total // 2
    groups = shard // GROUP
    panel_tiles = sum(place[2] for place in places)
    scalars = pl.BlockSpec(memory_space=pltpu.SMEM)
    far = pl.BlockSpec(memory_space=pltpu.HBM)
    message = jax.ShapeDtypeStruct((chips, groups // 2, message_rows(k), order), jnp.int16)
    return pl.pallas_call(
        functools.partial(product_kernel, places, shard),
        out_shape=(jax.ShapeDtypeStruct((chips, shard, k, order), jnp.float32), message, message),
        in_specs=[scalars] * 3 + [far] * (len(pieces) + 1),
        out_specs=(far, far, far),
        scratch_shapes=[
            pltpu.VMEM((panel_tiles, k, order), jnp.bfloat16),
            pltpu.VMEM((slots, order, order), jnp.bfloat16),
            pltpu.VMEM((col_total * shard + 1, k, order), jnp.float32),
            pltpu.VMEM((chips, groups, message_rows(k), order), jnp.int16),
            pltpu.SemaphoreType.DMA((len(places),)),
            pltpu.SemaphoreType.DMA((slots // STEP,)),
            pltpu.SemaphoreType.DMA((chips,)),
            pltpu.SemaphoreType.DMA((2, chips)),
        ],
        compiler_params=pltpu.CompilerParams(vmem_limit_bytes=VMEM_LIMIT),
        name="block_product",
    )(block_rows, block_cols, counts, *pieces, blocks)


def combine_kernel(half, which, gates, form, own, sib, *refs):
    arrived = refs[: len(gates)]
    result, near_own, near, out, in_sem, out_sem = refs[-6:]
    groups, tiles, k, order = near_own.shape
    chip = lax.axis_index("col") // 2
    d = which(chip)
    first = half * groups

    def copies(g):
        sources = [sib.at[d, g]] + [ref.at[g] for ref in arrived]
        span = pl.ds((first + g) * tiles, tiles)
        return [pltpu.make_async_copy(own.at[d, span], near_own.at[g], in_sem.at[g, 0])] + [
            pltpu.make_async_copy(ref, near.at[i, g], in_sem.at[g, i + 1]) for i, ref in enumerate(sources)
        ]

    def out_copy(g):
        at = first + g
        if form == "message":
            there = result.at[g]
        elif form == "tiles":
            there = result.at[pl.ds(at * tiles, tiles)]
        else:
            there = result.at[:, pl.ds(at * tiles * order, tiles * order)]
        return pltpu.make_async_copy(out.at[g], there, out_sem.at[g])

    for g in range(groups):
        for copy in copies(g):
            copy.start()
    for g in range(groups):
        for copy in copies(g):
            copy.wait()
        parts = [decoder(near.at[0, g], k)]
        for i, gate in enumerate(gates):
            factor = None if gate is None else jnp.where(gate(chip), 1.0, 0.0)
            parts.append(decoder(near.at[i + 1, g], k, factor))
        sums = []
        for i in range(tiles):
            tile = near_own[g, i]
            for part in parts:
                tile = tile + part(i)
            if form == "message":
                sums.append(tile)
            elif form == "tiles":
                out[g, i] = tile.astype(out.dtype)
            else:
                out[g, :, i * order : (i + 1) * order] = tile
        if form == "message":
            encode(sums, out.at[g])
        out_copy(g).start()
    for g in range(groups):
        out_copy(g).wait()


def combine(half, which, own, sib, arrived, gates, form, into=None):
    _, shard, k, order = own.shape
    groups = sib.shape[1]
    rows = message_rows(k)
    far = pl.BlockSpec(memory_space=pltpu.HBM)
    if form == "message":
        out_shape = jax.ShapeDtypeStruct((groups, rows, order), jnp.int16)
        held = pltpu.VMEM((groups, rows, order), jnp.int16)
    elif form == "tiles":
        out_shape = jax.ShapeDtypeStruct((shard, k, order), jnp.bfloat16)
        held = pltpu.VMEM((groups, GROUP, k, order), jnp.bfloat16)
    else:
        out_shape = jax.ShapeDtypeStruct((k, shard * order), jnp.float32)
        held = pltpu.VMEM((groups, k, GROUP * order), jnp.float32)
    operands = (own, sib, *arrived) + (() if into is None else (into,))
    return pl.pallas_call(
        functools.partial(combine_kernel, half, which, gates, form),
        out_shape=out_shape,
        in_specs=[far] * len(operands),
        out_specs=far,
        input_output_aliases={} if into is None else {len(operands) - 1: 0},
        scratch_shapes=[
            pltpu.VMEM((groups, GROUP, k, order), jnp.float32),
            pltpu.VMEM((1 + len(arrived), groups, rows, order), jnp.int16),
            held,
            pltpu.SemaphoreType.DMA((groups, 2 + len(arrived))),
            pltpu.SemaphoreType.DMA((groups,)),
        ],
        name="combine_" + form,
    )(*operands)


def chip_moves(moves):
    return [(2 * a + core, 2 * b + core) for a, b in moves for core in range(2)]


def is_end(chip):
    return (chip == 0) | (chip == 3)


def is_inner(chip):
    return (chip == 1) | (chip == 2)


def line_sum(half, own, msg, form, into):
    chips = own.shape[0]
    sib = lax.ppermute(msg, "col", [(c, c ^ 1) for c in range(2 * chips)])
    if chips == 4:
        send = combine(half, lambda z: 3 - 3 * (z % 2), own, sib, (), (), "message")
        got_a = lax.ppermute(send, "col", chip_moves([(0, 1), (1, 0), (2, 3), (3, 2)]))
        send = combine(half, lambda z: z ^ 2, own, sib, (got_a,), (is_inner,), "message")
        got_b = lax.ppermute(send, "col", chip_moves([(0, 1), (3, 2), (1, 3), (2, 0)]))
        send = combine(half, lambda z: 1 + z % 2, own, sib, (got_b,), (is_inner,), "message")
        got_c = lax.ppermute(send, "col", chip_moves([(0, 1), (3, 2)]))
        got_d = lax.ppermute(send, "col", chip_moves([(1, 2), (2, 1)]))
        arrived, gates = (got_a, got_b, got_c, got_d), (is_end, is_end, None, None)
    else:
        arrived = ()
        for step in range(1, chips):
            send = combine(half, lambda z: (z + step) % chips, own, sib, (), (), "message")
            moves = chip_moves([(a, (a + step) % chips) for a in range(chips)])
            arrived += (lax.ppermute(send, "col", moves),)
        gates = (None,) * len(arrived)
    return combine(half, lambda z: z, own, sib, arrived, gates, form, into)


def sum_over_col(partial, form):
    own, low, high = partial
    return line_sum(1, own, high, form, line_sum(0, own, low, form, None))


def gather_square(low, high):
    across_x = [(r, r ^ 1) for r in range(4)]
    across_y = [(r, r ^ 2) for r in range(4)]
    y_low = lax.ppermute(low, "row", across_y)
    x_high = lax.ppermute(high, "row", across_x)
    x_low = lax.ppermute(low, "row", across_x)
    y_high = lax.ppermute(high, "row", across_y)
    far_low = lax.ppermute(y_low, "row", across_x)
    far_high = lax.ppermute(x_high, "row", across_y)
    return low, high, x_low, x_high, y_low, y_high, far_low, far_high


def vector_panel(tiles, row_total):
    shard = tiles.shape[0]
    if row_total != 4:
        whole = lax.all_gather(tiles, "row", axis=0, tiled=True)
        return (whole,), ((0, 0, row_total * shard, lambda r: 0),)
    half = shard // 2
    places = []
    for piece in range(8):
        at = lambda r, piece=piece: (r ^ (piece // 2)) * shard + piece % 2 * half
        places.append((piece, 0, half, at))
    return gather_square(tiles[:half], tiles[half:]), tuple(places)


def first_panel(tiles, row_total, col_total):
    shard = tiles.shape[0]
    if (row_total, col_total) != (4, 8):
        moves = []
        for s in range(row_total * col_total):
            moves.append((s, (s % row_total) * col_total + s // row_total))
        return vector_panel(lax.ppermute(tiles, ("row", "col"), moves), row_total)
    quarter = shard // 4
    place = lax.axis_index("col") % 4
    got = []
    for j in range(4):
        moves = []
        for r in range(4):
            for c in range(8):
                moves.append((r * 8 + c, (c % 4 ^ j) * 8 + 2 * r + c // 4))
        part = lax.dynamic_slice_in_dim(tiles, (place ^ j) * quarter, quarter, 0)
        got.append(lax.ppermute(part, ("row", "col"), moves))
    places = []
    for piece in range(8):
        for i in range(2):

            def at(r, flip=piece // 2, j=piece % 2 * 2 + i):
                owner = r ^ flip
                return (owner ^ j) * shard + owner * quarter

            places.append((piece, i * quarter, quarter, at))
    low, high = jnp.concatenate(got[:2], axis=0), jnp.concatenate(got[2:], axis=0)
    return gather_square(low, high), tuple(places)


def shards(row_total, col_total, vectors, blocks, block_rows, block_cols, counts):
    k, width = vectors.shape
    order = blocks.shape[2]
    shard = width // order
    matrix = (blocks[0], block_rows, block_cols, counts, shard, col_total)
    tiles = vectors.reshape(k, shard, order).transpose(1, 0, 2)
    first = sum_over_col(block_product(*vector_panel(tiles, row_total), *matrix), "tiles")
    return sum_over_col(block_product(*first_panel(first, row_total, col_total), *matrix), "rows")


def solution(mesh):
    in_specs = (
        P(None, ("col", "row")),
        P("row", "col", None, None),
        P("row", "col"),
        P("row", "col"),
        P("row", "col"),
    )
    out_specs = P(None, ("row", "col"))
    body = functools.partial(shards, mesh.shape["row"], mesh.shape["col"])
    return jax.shard_map(body, mesh=mesh, in_specs=in_specs, out_specs=out_specs, check_vma=False)
```

```python
import functools

import jax
import jax.numpy as jnp
from jax import lax
from jax.experimental import pallas as pl
from jax.experimental.pallas import tpu as pltpu
from jax.sharding import PartitionSpec as P

GROUP = 8
STEP = 32
TOP = 14.0
VMEM_LIMIT = 24 * 1024 * 1024

def message_rows(vec_width):
    return GROUP * vec_width + 16


def encode(tiles, ref):
    k = tiles[0].shape[0]
    exponents = []
    for i, tile in enumerate(tiles):
        peak = jnp.max(jnp.abs(tile), axis=0, keepdims=True)
        exponent = jnp.ceil(jnp.log2(jnp.maximum(peak, 1e-30)))
        scaled = jnp.round(tile * jnp.exp2(TOP - exponent))
        ref[i * k : (i + 1) * k, :] = scaled.astype(jnp.int32).astype(jnp.int16)
        exponents.append(exponent)
    rest = jnp.zeros((16 - len(tiles), tiles[0].shape[1]), jnp.float32)
    table = jnp.concatenate(exponents + [rest], axis=0)
    ref[len(tiles) * k :, :] = table.astype(jnp.int32).astype(jnp.int16)


def decoder(ref, k, factor=None):
    table = ref[GROUP * k :, :].astype(jnp.int32).astype(jnp.float32)
    scale = jnp.exp2(table - TOP)
    if factor is not None:
        scale = scale * factor

    def tile(i):
        codes = ref[i * k : (i + 1) * k, :].astype(jnp.int32).astype(jnp.float32)
        return codes * scale[i : i + 1, :]

    return tile


def near(x):
    return pltpu.with_memory_space_constraint(x, pltpu.VMEM)


NEAR = pl.BlockSpec(memory_space=pltpu.VMEM)
FAR = pl.BlockSpec(memory_space=pltpu.HBM)


def product_kernel(places, shard, rows, cols, count, *refs):
    total = len(refs) - 8
    pieces = refs[:total]
    blocks, acc, msg_low, msg_high, panel, held, piece_sem, block_sem = refs[total:]
    chips, groups = msg_low.shape[:2]
    k = panel.shape[1]
    row_total = acc.shape[0] - 1
    slots = blocks.shape[0]
    n = count[0, 0]
    row_owner, col_owner = lax.axis_index("row"), lax.axis_index("col")

    def piece_copy(i):
        piece, start, tiles, at = places[i]
        there = panel.at[pl.ds(at(row_owner, col_owner // 2), tiles)]
        return pltpu.make_async_copy(pieces[piece].at[pl.ds(start, tiles)], there, piece_sem.at[i])

    def block_copy(i):
        span = pl.ds(i * STEP, STEP)
        return pltpu.make_async_copy(blocks.at[span], held.at[span], block_sem.at[i])

    for i in range(len(places)):
        piece_copy(i).start()
    for i in range(slots // STEP):

        @pl.when(i * STEP < n)
        def _():
            block_copy(i).start()

    @pl.loop(0, row_total + 1)
    def _(i):
        acc[i] = jnp.zeros_like(acc[0])

    for i in range(len(places)):
        piece_copy(i).wait()

    @pl.loop(0, (n + STEP - 1) // STEP)
    def _(step):
        block_copy(step).wait()
        base = step * STEP
        nil = jnp.zeros(panel.shape[1:], panel.dtype)
        products = []
        for u in range(0, STEP, 2):
            upper = jnp.concatenate([panel[cols[0, base + u]], nil], axis=1)
            lower = jnp.concatenate([nil, panel[cols[0, base + u + 1]]], axis=1)
            both = lax.dot_general(
                jnp.concatenate([upper, lower], axis=0),
                jnp.concatenate([held[base + u], held[base + u + 1]], axis=1),
                (((1,), (1,)), ((), ())),
                preferred_element_type=jnp.float32,
            )
            products += [both[:k], both[k:]]
        for u in range(STEP):
            at = jnp.where(base + u < n, rows[0, base + u], row_total)
            acc[at] += products[u]

    other = 1 - col_owner % 2
    for half, msg in enumerate((msg_low, msg_high)):

        @pl.loop(0, chips * groups)
        def _(i):
            d, g = i // groups, i % groups
            base = (2 * d + other) * shard + (half * groups + g) * GROUP
            encode([acc[base + t] for t in range(GROUP)], msg.at[d, g])


def block_product(pieces, places, blocks, block_rows, block_cols, counts, shard, col_total):
    slots, order, _ = blocks.shape
    k = pieces[0].shape[1]
    panel_tiles = sum(place[2] for place in places)
    scalars = pl.BlockSpec(memory_space=pltpu.SMEM)
    message = pltpu.VMEM((col_total // 2, shard // GROUP // 2, message_rows(k), order), jnp.int16)
    return pl.pallas_call(
        functools.partial(product_kernel, places, shard),
        out_shape=(pltpu.VMEM((col_total * shard + 1, k, order), jnp.float32), message, message),
        in_specs=[scalars] * 3 + [NEAR] * len(pieces) + [FAR],
        out_specs=(NEAR, NEAR, NEAR),
        scratch_shapes=[
            pltpu.VMEM((panel_tiles, k, order), jnp.bfloat16),
            pltpu.VMEM((slots, order, order), jnp.bfloat16),
            pltpu.SemaphoreType.DMA((len(places),)),
            pltpu.SemaphoreType.DMA((slots // STEP,)),
        ],
        compiler_params=pltpu.CompilerParams(vmem_limit_bytes=VMEM_LIMIT),
        name="block_product",
    )(block_rows, block_cols, counts, *[near(p) for p in pieces], pltpu.with_memory_space_constraint(blocks, pltpu.HBM))


def combine_kernel(half, which, gates, form, acc, sib, *refs):
    arrived = refs[: len(gates)]
    chips, groups = sib.shape[:2]
    _, k, order = acc.shape
    shard = acc.shape[0] // (2 * chips)
    col_owner = lax.axis_index("col")
    chip = col_owner // 2
    d = which(chip)
    base = (2 * d + col_owner % 2) * shard + half * groups * GROUP
    if form == "rows":
        result, out, out_sem = refs[-3:]
    elif form == "message":
        result = refs[-1]
    results = refs[len(gates) :]
    step = results[0].shape[0]

    def out_copy(g):
        width = GROUP * order
        there = result.at[:, pl.ds((half * groups + g) * width, width)]
        return pltpu.make_async_copy(out.at[g], there, out_sem.at[g])

    for g in range(groups):
        parts = [decoder(sib.at[d, g], k)]
        for ref, gate in zip(arrived, gates):
            factor = None if gate is None else jnp.where(gate(chip), 1.0, 0.0)
            parts.append(decoder(ref.at[g], k, factor))
        sums = []
        for i in range(GROUP):
            tile = acc[base + g * GROUP + i]
            for part in parts:
                tile = tile + part(i)
            if form == "message":
                sums.append(tile)
            elif form == "tiles":
                at = g * GROUP + i
                results[at // step][at % step] = tile.astype(results[0].dtype)
            else:
                out[g, :, i * order : (i + 1) * order] = tile
        if form == "message":
            encode(sums, result.at[g])
        elif form == "rows":
            out_copy(g).start()
    if form == "rows":
        for g in range(groups):
            out_copy(g).wait()


def combine(half, which, acc, sib, arrived, gates, form, into=None):
    chips, groups, rows, order = sib.shape
    k = acc.shape[1]
    operands = [near(x) for x in (acc, sib, *arrived)]
    specs = [NEAR] * len(operands)
    aliases, scratch, out_spec = {}, [], NEAR
    if form == "message":
        out_shape = pltpu.VMEM((groups, rows, order), jnp.int16)
    elif form == "tiles":
        parts = 4 if groups * GROUP % 4 == 0 else 1
        out_shape = (pltpu.VMEM((groups * GROUP // parts, k, order), jnp.bfloat16),) * parts
        out_spec = (NEAR,) * parts
    else:
        shard = acc.shape[0] // (2 * chips)
        out_shape = jax.ShapeDtypeStruct((k, shard * order), jnp.float32)
        out_spec = FAR
        scratch = [pltpu.VMEM((groups, k, GROUP * order), jnp.float32), pltpu.SemaphoreType.DMA((groups,))]
        if into is not None:
            aliases = {len(operands): 0}
            operands.append(into)
            specs.append(FAR)
    return pl.pallas_call(
        functools.partial(combine_kernel, half, which, gates, form),
        out_shape=out_shape,
        in_specs=specs,
        out_specs=out_spec,
        input_output_aliases=aliases,
        scratch_shapes=scratch,
        compiler_params=pltpu.CompilerParams(vmem_limit_bytes=4 * 1024 * 1024),
        name="combine_" + form,
    )(*operands)


def chip_moves(moves):
    return [(2 * a + core, 2 * b + core) for a, b in moves for core in range(2)]


def is_end(chip):
    return (chip == 0) | (chip == 3)


def is_inner(chip):
    return (chip == 1) | (chip == 2)


def line_sum(half, acc, msg, form, into=None):
    chips = msg.shape[0]
    sib = lax.ppermute(msg, "col", [(c, c ^ 1) for c in range(2 * chips)])
    if chips == 4:
        send = combine(half, lambda z: 3 - 3 * (z % 2), acc, sib, (), (), "message")
        got_a = lax.ppermute(send, "col", chip_moves([(0, 1), (1, 0), (2, 3), (3, 2)]))
        send = combine(half, lambda z: z ^ 2, acc, sib, (got_a,), (is_inner,), "message")
        got_b = lax.ppermute(send, "col", chip_moves([(0, 1), (3, 2), (1, 3), (2, 0)]))
        send = combine(half, lambda z: 1 + z % 2, acc, sib, (got_b,), (is_inner,), "message")
        got_c = lax.ppermute(send, "col", chip_moves([(0, 1), (3, 2)]))
        got_d = lax.ppermute(send, "col", chip_moves([(1, 2), (2, 1)]))
        arrived, gates = (got_a, got_b, got_c, got_d), (is_end, is_end, None, None)
    else:
        arrived = ()
        for step in range(1, chips):
            send = combine(half, lambda z: (z + step) % chips, acc, sib, (), (), "message")
            moves = chip_moves([(a, (a + step) % chips) for a in range(chips)])
            arrived += (lax.ppermute(send, "col", moves),)
        gates = (None,) * len(arrived)
    return combine(half, lambda z: z, acc, sib, arrived, gates, form, into)


def across(x, flip):
    return lax.ppermute(x, "row", [(r, r ^ flip) for r in range(4)])


def gather_square(low, high):
    y_low = across(low, 2)
    x_high = across(high, 1)
    x_low = across(low, 1)
    y_high = across(high, 2)
    return low, high, x_low, x_high, y_low, y_high, across(y_low, 1), across(x_high, 2)


def vector_panel(tiles, row_total):
    shard = tiles.shape[0]
    if row_total != 4:
        whole = lax.all_gather(tiles, "row", axis=0, tiled=True)
        return (whole,), ((0, 0, row_total * shard, lambda r, z: 0),)
    half = shard // 2
    places = []
    for piece in range(8):
        at = lambda r, z, piece=piece: (r ^ (piece // 2)) * shard + piece % 2 * half
        places.append((piece, 0, half, at))
    return gather_square(tiles[:half], tiles[half:]), tuple(places)


def shuffle_kernel(pick, *refs):
    half = len(refs) // 2
    for i in range(half):
        wanted = pick(lax.axis_index("row"), lax.axis_index("col"), i)
        for j in range(half):

            @pl.when(wanted == j)
            def _():
                refs[half + i][...] = refs[j][...]


def shuffle(parts, pick):
    return pl.pallas_call(
        functools.partial(shuffle_kernel, pick),
        out_shape=tuple(pltpu.VMEM(x.shape, x.dtype) for x in parts),
        in_specs=[NEAR] * len(parts),
        out_specs=(NEAR,) * len(parts),
        compiler_params=pltpu.CompilerParams(vmem_limit_bytes=1024 * 1024),
        name="shuffle",
    )(*[near(x) for x in parts])


def join_kernel(*refs):
    step = refs[0].shape[0]
    for i, ref in enumerate(refs[:-1]):
        refs[-1][i * step : (i + 1) * step] = ref[...]


def join(parts):
    shape = (len(parts) * parts[0].shape[0],) + parts[0].shape[1:]
    return pl.pallas_call(
        join_kernel,
        out_shape=pltpu.VMEM(shape, parts[0].dtype),
        in_specs=[NEAR] * len(parts),
        out_specs=NEAR,
        compiler_params=pltpu.CompilerParams(vmem_limit_bytes=1024 * 1024),
        name="join",
    )(*[near(x) for x in parts])


def spread(quarters):
    parts = shuffle(quarters, lambda r, c, i: r ^ i)
    parts = parts[:1] + tuple(across(parts[f], f) for f in (1, 2, 3))
    parts = shuffle(parts, lambda r, c, i: r ^ (c % 4) ^ i)
    got = []
    for j in range(4):
        got.append(lax.ppermute(parts[j], "col", [(c, 2 * (c % 4 ^ j) + c // 4) for c in range(8)]))
    return join(got)


def first_panel(low, high, row_total, col_total):
    if (row_total, col_total) != (4, 8):
        moves = []
        for s in range(row_total * col_total):
            moves.append((s, (s % row_total) * col_total + s // row_total))
        tiles = lax.ppermute(jnp.concatenate(low + high, axis=0), ("row", "col"), moves)
        return vector_panel(tiles, row_total)
    quarter = low[0].shape[0]
    places = []
    for piece in range(8):
        for j in range(4):

            def at(r, z, flip=piece // 2, which=piece % 2, j=j):
                return (z ^ j) * 8 * quarter + which * 4 * quarter + (r ^ flip) * quarter

            places.append((piece, j * quarter, quarter, at))
    return gather_square(spread(low), spread(high)), tuple(places)


def shards(row_total, col_total, vectors, blocks, block_rows, block_cols, counts):
    k, width = vectors.shape
    order = blocks.shape[2]
    shard = width // order
    matrix = (blocks[0], block_rows, block_cols, counts, shard, col_total)
    tiles = vectors.reshape(k, shard, order).transpose(1, 0, 2)
    acc, low, high = block_product(*vector_panel(tiles, row_total), *matrix)
    firsts = line_sum(0, acc, low, "tiles"), line_sum(1, acc, high, "tiles")
    acc, low, high = block_product(*first_panel(*firsts, row_total, col_total), *matrix)
    return line_sum(1, acc, high, "rows", line_sum(0, acc, low, "rows"))


def solution(mesh):
    in_specs = (
        P(None, ("col", "row")),
        P("row", "col", None, None),
        P("row", "col"),
        P("row", "col"),
        P("row", "col"),
    )
    out_specs = P(None, ("row", "col"))
    body = functools.partial(shards, mesh.shape["row"], mesh.shape["col"])
    return jax.shard_map(body, mesh=mesh, in_specs=in_specs, out_specs=out_specs, check_vma=False)
```

```python
import functools

import jax
import jax.numpy as jnp
from jax import lax
from jax.experimental import pallas as pl
from jax.experimental.pallas import tpu as pltpu
from jax.sharding import PartitionSpec as P

GROUP = 8
STEP = 32
TOP = 14.0
SMALL = 4 * 1024 * 1024

def message_rows(vec_width):
    return GROUP * vec_width + 16


def encode(tiles, ref):
    k = tiles[0].shape[0]
    exponents = []
    for i, tile in enumerate(tiles):
        peak = jnp.max(jnp.abs(tile), axis=0, keepdims=True)
        exponent = jnp.ceil(jnp.log2(jnp.maximum(peak, 1e-30)))
        scaled = jnp.round(tile * jnp.exp2(TOP - exponent))
        ref[i * k : (i + 1) * k, :] = scaled.astype(jnp.int32).astype(jnp.int16)
        exponents.append(exponent)
    rest = jnp.zeros((16 - len(tiles), tiles[0].shape[1]), jnp.float32)
    table = jnp.concatenate(exponents + [rest], axis=0)
    ref[len(tiles) * k :, :] = table.astype(jnp.int32).astype(jnp.int16)


def decoder(ref, k, factor=None):
    table = ref[GROUP * k :, :].astype(jnp.int32).astype(jnp.float32)
    scale = jnp.exp2(table - TOP)
    if factor is not None:
        scale = scale * factor

    def tile(i):
        codes = ref[i * k : (i + 1) * k, :].astype(jnp.int32).astype(jnp.float32)
        return codes * scale[i : i + 1, :]

    return tile


def near(x):
    return pltpu.with_memory_space_constraint(x, pltpu.VMEM)


NEAR = pl.BlockSpec(memory_space=pltpu.VMEM)
FAR = pl.BlockSpec(memory_space=pltpu.HBM)


def prepare_kernel(load, count, *refs):
    total = len(refs) - (5 if load else 3)
    pieces = refs[:total]
    if load:
        blocks, panel, acc, held, sem = refs[total:]
        slots = blocks.shape[0]
        n = count[0, 0]

        def block_copy(i):
            span = pl.ds(i * STEP, STEP)
            return pltpu.make_async_copy(blocks.at[span], held.at[span], sem.at[i])

        for i in range(slots // STEP):

            @pl.when(i * STEP < n)
            def _():
                block_copy(i).start()
    else:
        panel, acc, sem = refs[total:]

    def piece_copy(i):
        tiles = pieces[i].shape[0]
        return pltpu.make_async_copy(pieces[i], panel.at[pl.ds(i * tiles, tiles)], sem.at[sem.shape[0] - 1 - i])

    for i in range(total):
        piece_copy(i).start()

    @pl.loop(0, acc.shape[0])
    def _(i):
        acc[i] = jnp.zeros_like(acc[0])

    for i in range(total):
        piece_copy(i).wait()
    if load:
        for i in range(slots // STEP):

            @pl.when(i * STEP < n)
            def _():
                block_copy(i).wait()


def prepare(pieces, panel_tiles, acc_tiles, k, order, counts, blocks=None):
    operands = [near(p) for p in pieces]
    specs = [pl.BlockSpec(memory_space=pltpu.SMEM)] + [NEAR] * len(pieces)
    out_shape = [
        pltpu.VMEM((panel_tiles, k, order), jnp.bfloat16),
        pltpu.VMEM((acc_tiles, k, order), jnp.float32),
    ]
    copies = len(pieces)
    if blocks is not None:
        operands.append(pltpu.with_memory_space_constraint(blocks, pltpu.HBM))
        specs.append(FAR)
        out_shape.append(pltpu.VMEM(blocks.shape, blocks.dtype))
        copies += blocks.shape[0] // STEP
    return pl.pallas_call(
        functools.partial(prepare_kernel, blocks is not None),
        out_shape=tuple(out_shape),
        in_specs=specs,
        out_specs=(NEAR,) * len(out_shape),
        scratch_shapes=[pltpu.SemaphoreType.DMA((max(copies, 1),))],
        compiler_params=pltpu.CompilerParams(vmem_limit_bytes=SMALL),
        name="prepare",
    )(counts, *operands)


def product_kernel(place, shard, rows, cols, count, panel_in, acc_in, held, *refs):
    total = len(refs) - 5
    pieces = refs[:total]
    panel, acc, msg_low, msg_high, sem = refs[total:]
    chips, groups = msg_low.shape[:2]
    k = panel.shape[1]
    row_total = acc.shape[0] - 1
    n = count[0, 0]
    row_owner, col_owner = lax.axis_index("row"), lax.axis_index("col")

    def piece_copy(i):
        tiles = pieces[i].shape[0]
        start = panel.shape[0] - (total - i) * tiles
        return pltpu.make_async_copy(pieces[i], panel.at[pl.ds(start, tiles)], sem.at[i])

    for i in range(total):
        piece_copy(i).start()
    for i in range(total):
        piece_copy(i).wait()

    @pl.loop(0, (n + STEP - 1) // STEP)
    def _(step):
        base = step * STEP
        nil = jnp.zeros(panel.shape[1:], panel.dtype)

        def entry(u):
            return panel[place(cols[0, base + u], row_owner, col_owner // 2)]

        products = []
        for u in range(0, STEP, 2):
            upper = jnp.concatenate([entry(u), nil], axis=1)
            lower = jnp.concatenate([nil, entry(u + 1)], axis=1)
            both = lax.dot_general(
                jnp.concatenate([upper, lower], axis=0),
                jnp.concatenate([held[base + u], held[base + u + 1]], axis=1),
                (((1,), (1,)), ((), ())),
                preferred_element_type=jnp.float32,
            )
            products += [both[:k], both[k:]]
        for u in range(STEP):
            at = jnp.where(base + u < n, rows[0, base + u], row_total)
            acc[at] += products[u]

    other = 1 - col_owner % 2
    for half, msg in enumerate((msg_low, msg_high)):

        @pl.loop(0, chips * groups)
        def _(i):
            d, g = i // groups, i % groups
            base = (2 * d + other) * shard + (half * groups + g) * GROUP
            encode([acc[base + t] for t in range(GROUP)], msg.at[d, g])


def block_product(late, place, panel, acc, held, block_rows, block_cols, counts, shard, col_total):
    _, k, order = panel.shape
    scalars = pl.BlockSpec(memory_space=pltpu.SMEM)
    message = pltpu.VMEM((col_total // 2, shard // GROUP // 2, message_rows(k), order), jnp.int16)
    return pl.pallas_call(
        functools.partial(product_kernel, place, shard),
        out_shape=(pltpu.VMEM(panel.shape, panel.dtype), pltpu.VMEM(acc.shape, acc.dtype), message, message),
        in_specs=[scalars] * 3 + [NEAR] * (3 + len(late)),
        out_specs=(NEAR,) * 4,
        input_output_aliases={3: 0, 4: 1},
        scratch_shapes=[pltpu.SemaphoreType.DMA((max(len(late), 1),))],
        compiler_params=pltpu.CompilerParams(vmem_limit_bytes=SMALL),
        name="block_product",
    )(block_rows, block_cols, counts, near(panel), near(acc), near(held), *[near(p) for p in late])[1:]


def combine_kernel(half, which, gates, form, acc, sib, *refs):
    arrived = refs[: len(gates)]
    chips, groups = sib.shape[:2]
    _, k, order = acc.shape
    shard = acc.shape[0] // (2 * chips)
    col_owner = lax.axis_index("col")
    chip = col_owner // 2
    d = which(chip)
    base = (2 * d + col_owner % 2) * shard + half * groups * GROUP
    if form == "rows":
        result, out, out_sem = refs[-3:]
    elif form == "message":
        result = refs[-1]
    results = refs[len(gates) :]
    step = results[0].shape[0]

    def out_copy(g):
        width = GROUP * order
        there = result.at[:, pl.ds((half * groups + g) * width, width)]
        return pltpu.make_async_copy(out.at[g], there, out_sem.at[g])

    for g in range(groups):
        parts = [decoder(sib.at[d, g], k)]
        for ref, gate in zip(arrived, gates):
            factor = None if gate is None else jnp.where(gate(chip), 1.0, 0.0)
            parts.append(decoder(ref.at[g], k, factor))
        sums = []
        for i in range(GROUP):
            tile = acc[base + g * GROUP + i]
            for part in parts:
                tile = tile + part(i)
            if form == "message":
                sums.append(tile)
            elif form == "tiles":
                at = g * GROUP + i
                results[at // step][at % step] = tile.astype(results[0].dtype)
            else:
                out[g, :, i * order : (i + 1) * order] = tile
        if form == "message":
            encode(sums, result.at[g])
        elif form == "rows":
            out_copy(g).start()
    if form == "rows":
        for g in range(groups):
            out_copy(g).wait()


def combine(half, which, acc, sib, arrived, gates, form, into=None):
    chips, groups, rows, order = sib.shape
    k = acc.shape[1]
    operands = [near(x) for x in (acc, sib, *arrived)]
    specs = [NEAR] * len(operands)
    aliases, scratch, out_spec = {}, [], NEAR
    if form == "message":
        out_shape = pltpu.VMEM((groups, rows, order), jnp.int16)
    elif form == "tiles":
        parts = 4 if groups * GROUP % 4 == 0 else 1
        out_shape = (pltpu.VMEM((groups * GROUP // parts, k, order), jnp.bfloat16),) * parts
        out_spec = (NEAR,) * parts
    else:
        shard = acc.shape[0] // (2 * chips)
        out_shape = jax.ShapeDtypeStruct((k, shard * order), jnp.float32)
        out_spec = FAR
        scratch = [pltpu.VMEM((groups, k, GROUP * order), jnp.float32), pltpu.SemaphoreType.DMA((groups,))]
        if into is not None:
            aliases = {len(operands): 0}
            operands.append(into)
            specs.append(FAR)
    return pl.pallas_call(
        functools.partial(combine_kernel, half, which, gates, form),
        out_shape=out_shape,
        in_specs=specs,
        out_specs=out_spec,
        input_output_aliases=aliases,
        scratch_shapes=scratch,
        compiler_params=pltpu.CompilerParams(vmem_limit_bytes=SMALL),
        name="combine_" + form,
    )(*operands)


def chip_moves(moves):
    return [(2 * a + core, 2 * b + core) for a, b in moves for core in range(2)]


def is_end(chip):
    return (chip == 0) | (chip == 3)


def is_inner(chip):
    return (chip == 1) | (chip == 2)


def line_sum(half, acc, msg, form, into=None):
    chips = msg.shape[0]
    sib = lax.ppermute(msg, "col", [(c, c ^ 1) for c in range(2 * chips)])
    if chips == 4:
        send = combine(half, lambda z: 3 - 3 * (z % 2), acc, sib, (), (), "message")
        got_a = lax.ppermute(send, "col", chip_moves([(0, 1), (1, 0), (2, 3), (3, 2)]))
        send = combine(half, lambda z: z ^ 2, acc, sib, (got_a,), (is_inner,), "message")
        got_b = lax.ppermute(send, "col", chip_moves([(0, 1), (3, 2), (1, 3), (2, 0)]))
        send = combine(half, lambda z: 1 + z % 2, acc, sib, (got_b,), (is_inner,), "message")
        got_c = lax.ppermute(send, "col", chip_moves([(0, 1), (3, 2)]))
        got_d = lax.ppermute(send, "col", chip_moves([(1, 2), (2, 1)]))
        arrived, gates = (got_a, got_b, got_c, got_d), (is_end, is_end, None, None)
    else:
        arrived = ()
        for step in range(1, chips):
            send = combine(half, lambda z: (z + step) % chips, acc, sib, (), (), "message")
            moves = chip_moves([(a, (a + step) % chips) for a in range(chips)])
            arrived += (lax.ppermute(send, "col", moves),)
        gates = (None,) * len(arrived)
    return combine(half, lambda z: z, acc, sib, arrived, gates, form, into)


def across(x, flip):
    return lax.ppermute(x, "row", [(r, r ^ flip) for r in range(4)])


def gather_square(low, high):
    y_low = across(low, 2)
    x_high = across(high, 1)
    x_low = across(low, 1)
    y_high = across(high, 2)
    return low, high, x_low, x_high, y_low, y_high, across(y_low, 1), across(x_high, 2)


def vector_panel(tiles, row_total):
    shard = tiles.shape[0]
    if row_total != 4:
        return (lax.all_gather(tiles, "row", axis=0, tiled=True),), lambda c, r, z: c
    half = shard // 2
    return gather_square(tiles[:half], tiles[half:]), lambda c, r, z: c ^ (r * shard)


def shuffle_kernel(pick, merge, *refs):
    total = len(refs) * merge // (merge + 1)
    step = refs[0].shape[0]
    for i in range(total):
        wanted = pick(lax.axis_index("row"), lax.axis_index("col"), i)
        for j in range(total):

            @pl.when(wanted == j)
            def _():
                refs[total + i // merge][i % merge * step : (i % merge + 1) * step] = refs[j][...]


def shuffle(parts, pick, merge=1):
    shape = (merge * parts[0].shape[0],) + parts[0].shape[1:]
    return pl.pallas_call(
        functools.partial(shuffle_kernel, pick, merge),
        out_shape=(pltpu.VMEM(shape, parts[0].dtype),) * (len(parts) // merge),
        in_specs=[NEAR] * len(parts),
        out_specs=(NEAR,) * (len(parts) // merge),
        compiler_params=pltpu.CompilerParams(vmem_limit_bytes=SMALL),
        name="shuffle",
    )(*[near(x) for x in parts])


def spread(quarters):
    parts = shuffle(quarters, lambda r, c, i: (r // 2 * 2 + c % 2) ^ i)
    got = []
    for i in range(4):
        moves = []
        for r in range(4):
            for c in range(8):
                moves.append((r * 8 + c, ((r // 2 * 2 + c % 2) ^ i) * 8 + c // 2 * 2 + r % 2))
        got.append(lax.ppermute(parts[i], ("row", "col"), moves))
    pairs = shuffle(tuple(got), lambda r, c, i: r ^ (c // 2 % 2 * 2 ^ i), merge=2)
    got = []
    for i in range(2):
        moves = [(c, 2 * (c % 2 + 2 * (c // 2 % 2 ^ i)) + c // 4) for c in range(8)]
        got.append(lax.ppermute(pairs[i], "col", moves))
    return shuffle(tuple(got), lambda r, c, i: c // 4 ^ i, merge=2)[0]


def first_panel(low, high, row_total, col_total):
    if (row_total, col_total) != (4, 8):
        moves = []
        for s in range(row_total * col_total):
            moves.append((s, (s % row_total) * col_total + s // row_total))
        tiles = lax.ppermute(jnp.concatenate(low + high, axis=0), ("row", "col"), moves)
        return vector_panel(tiles, row_total)
    quarter = low[0].shape[0]

    def place(c, r, z):
        block, tile = lax.div(c, quarter), lax.rem(c, quarter)
        part, which, owner = block >> 3, (block >> 2) & 1, block & 3
        return ((((owner ^ r) * 2 + which) * 4) + part) * quarter + tile

    return gather_square(spread(low), spread(high)), place


def shards(row_total, col_total, vectors, blocks, block_rows, block_cols, counts):
    k, width = vectors.shape
    order = blocks.shape[2]
    shard = width // order
    sizes = (row_total * shard, col_total * shard + 1, k, order)
    index = (block_rows, block_cols, counts, shard, col_total)
    tiles = vectors.reshape(k, shard, order).transpose(1, 0, 2)
    pieces, place = vector_panel(tiles, row_total)
    early = len(pieces) * 3 // 4
    panel, acc, held = prepare(pieces[:early], *sizes, counts, blocks[0])
    acc, low, high = block_product(pieces[early:], place, panel, acc, held, *index)
    firsts = line_sum(0, acc, low, "tiles"), line_sum(1, acc, high, "tiles")
    pieces, place = first_panel(*firsts, row_total, col_total)
    panel, acc = prepare(pieces[:early], *sizes, counts)
    acc, low, high = block_product(pieces[early:], place, panel, acc, held, *index)
    return line_sum(1, acc, high, "rows", line_sum(0, acc, low, "rows"))


def solution(mesh):
    in_specs = (
        P(None, ("col", "row")),
        P("row", "col", None, None),
        P("row", "col"),
        P("row", "col"),
        P("row", "col"),
    )
    out_specs = P(None, ("row", "col"))
    body = functools.partial(shards, mesh.shape["row"], mesh.shape["col"])
    return jax.shard_map(body, mesh=mesh, in_specs=in_specs, out_specs=out_specs, check_vma=False)
```

```python
import functools

import jax
import jax.numpy as jnp
from jax import lax
from jax.experimental import pallas as pl
from jax.experimental.pallas import tpu as pltpu
from jax.sharding import PartitionSpec as P

GROUP = 8
STEP = 32
TOP = 14.0
SMALL = 4 * 1024 * 1024

def message_rows(vec_width):
    return GROUP * vec_width + 16


def encode(tiles, ref):
    k = tiles[0].shape[0]
    exponents = []
    for i, tile in enumerate(tiles):
        peak = jnp.max(jnp.abs(tile), axis=0, keepdims=True)
        exponent = jnp.ceil(jnp.log2(jnp.maximum(peak, 1e-30)))
        scaled = jnp.round(tile * jnp.exp2(TOP - exponent))
        ref[i * k : (i + 1) * k, :] = scaled.astype(jnp.int32).astype(jnp.int16)
        exponents.append(exponent)
    rest = jnp.zeros((16 - len(tiles), tiles[0].shape[1]), jnp.float32)
    table = jnp.concatenate(exponents + [rest], axis=0)
    ref[len(tiles) * k :, :] = table.astype(jnp.int32).astype(jnp.int16)


def decoder(ref, k, factor=None):
    table = ref[GROUP * k :, :].astype(jnp.int32).astype(jnp.float32)
    scale = jnp.exp2(table - TOP)
    if factor is not None:
        scale = scale * factor

    def tile(i):
        codes = ref[i * k : (i + 1) * k, :].astype(jnp.int32).astype(jnp.float32)
        return codes * scale[i : i + 1, :]

    return tile


def near(x):
    return pltpu.with_memory_space_constraint(x, pltpu.VMEM)


NEAR = pl.BlockSpec(memory_space=pltpu.VMEM)
FAR = pl.BlockSpec(memory_space=pltpu.HBM)


def prepare_kernel(load, count, *refs):
    total = len(refs) - (5 if load else 3)
    pieces = refs[:total]
    if load:
        blocks, panel, acc, held, sem = refs[total:]
        slots = blocks.shape[0]
        n = count[0, 0]

        def block_copy(i):
            span = pl.ds(i * STEP, STEP)
            return pltpu.make_async_copy(blocks.at[span], held.at[span], sem.at[i])

        for i in range(slots // STEP):

            @pl.when(i * STEP < n)
            def _():
                block_copy(i).start()
    else:
        panel, acc, sem = refs[total:]

    def piece_copy(i):
        tiles = pieces[i].shape[0]
        return pltpu.make_async_copy(pieces[i], panel.at[pl.ds(i * tiles, tiles)], sem.at[sem.shape[0] - 1 - i])

    for i in range(total):
        piece_copy(i).start()

    @pl.loop(0, acc.shape[0])
    def _(i):
        acc[i] = jnp.zeros_like(acc[0])

    for i in range(total):
        piece_copy(i).wait()
    if load:
        for i in range(slots // STEP):

            @pl.when(i * STEP < n)
            def _():
                block_copy(i).wait()


def prepare(pieces, panel_tiles, acc_tiles, k, order, counts, blocks=None):
    operands = [near(p) for p in pieces]
    specs = [pl.BlockSpec(memory_space=pltpu.SMEM)] + [NEAR] * len(pieces)
    out_shape = [
        pltpu.VMEM((panel_tiles, k, order), jnp.bfloat16),
        pltpu.VMEM((acc_tiles, k, order), jnp.float32),
    ]
    copies = len(pieces)
    if blocks is not None:
        operands.append(pltpu.with_memory_space_constraint(blocks, pltpu.HBM))
        specs.append(FAR)
        out_shape.append(pltpu.VMEM(blocks.shape, blocks.dtype))
        copies += blocks.shape[0] // STEP
    return pl.pallas_call(
        functools.partial(prepare_kernel, blocks is not None),
        out_shape=tuple(out_shape),
        in_specs=specs,
        out_specs=(NEAR,) * len(out_shape),
        scratch_shapes=[pltpu.SemaphoreType.DMA((max(copies, 1),))],
        compiler_params=pltpu.CompilerParams(vmem_limit_bytes=SMALL),
        name="prepare",
    )(counts, *operands)


def product_kernel(place, halves, shard, rows, cols, count, panel_in, acc_in, held, *refs):
    total = len(refs) - 5
    pieces = refs[:total]
    panel, acc, msg_low, msg_high, sem = refs[total:]
    chips, groups = msg_low.shape[:2]
    k = panel.shape[1]
    row_total = acc.shape[0] - 1
    n = count[0, 0]
    row_owner, col_owner = lax.axis_index("row"), lax.axis_index("col")

    def piece_copy(i):
        tiles = pieces[i].shape[0]
        start = panel.shape[0] - (total - i) * tiles
        return pltpu.make_async_copy(pieces[i], panel.at[pl.ds(start, tiles)], sem.at[i])

    for i in range(total):
        piece_copy(i).start()
    for i in range(total):
        piece_copy(i).wait()

    @pl.loop(0, (n + STEP - 1) // STEP)
    def _(step):
        base = step * STEP
        nil = jnp.zeros(panel.shape[1:], panel.dtype)

        def entry(u):
            return panel[place(cols[0, base + u], row_owner)]

        products = []
        for u in range(0, STEP, 2):
            upper = jnp.concatenate([entry(u), nil], axis=1)
            lower = jnp.concatenate([nil, entry(u + 1)], axis=1)
            both = lax.dot_general(
                jnp.concatenate([upper, lower], axis=0),
                jnp.concatenate([held[base + u], held[base + u + 1]], axis=1),
                (((1,), (1,)), ((), ())),
                preferred_element_type=jnp.float32,
            )
            products += [both[:k], both[k:]]
        for u in range(STEP):
            at = jnp.where(base + u < n, rows[0, base + u], row_total)
            acc[at] += products[u]

    other = 1 - col_owner % 2
    for half, msg in enumerate((msg_low, msg_high)):

        @pl.loop(0, chips * groups)
        def _(i):
            d, g = i // groups, i % groups
            owner = other * chips + d if halves else 2 * d + other
            base = owner * shard + (half * groups + g) * GROUP
            encode([acc[base + t] for t in range(GROUP)], msg.at[d, g])


def block_product(late, place, halves, panel, acc, held, block_rows, block_cols, counts, shard, col_total):
    _, k, order = panel.shape
    scalars = pl.BlockSpec(memory_space=pltpu.SMEM)
    message = pltpu.VMEM((col_total // 2, shard // GROUP // 2, message_rows(k), order), jnp.int16)
    return pl.pallas_call(
        functools.partial(product_kernel, place, halves, shard),
        out_shape=(pltpu.VMEM(panel.shape, panel.dtype), pltpu.VMEM(acc.shape, acc.dtype), message, message),
        in_specs=[scalars] * 3 + [NEAR] * (3 + len(late)),
        out_specs=(NEAR,) * 4,
        input_output_aliases={3: 0, 4: 1},
        scratch_shapes=[pltpu.SemaphoreType.DMA((max(len(late), 1),))],
        compiler_params=pltpu.CompilerParams(vmem_limit_bytes=SMALL),
        name="block_product",
    )(block_rows, block_cols, counts, near(panel), near(acc), near(held), *[near(p) for p in late])[1:]


def combine_kernel(half, which, gates, form, acc, sib, *refs):
    arrived = refs[: len(gates)]
    chips, groups = sib.shape[:2]
    _, k, order = acc.shape
    shard = acc.shape[0] // (2 * chips)
    col_owner = lax.axis_index("col")
    chip = col_owner // 2
    d = which(chip)
    base = (2 * d + col_owner % 2) * shard + half * groups * GROUP
    if form == "rows":
        result, out, out_sem = refs[-3:]
    else:
        result = refs[-1]

    def out_copy(g):
        width = GROUP * order
        there = result.at[:, pl.ds((half * groups + g) * width, width)]
        return pltpu.make_async_copy(out.at[g], there, out_sem.at[g])

    for g in range(groups):
        parts = [decoder(sib.at[d, g], k)]
        for ref, gate in zip(arrived, gates):
            factor = None if gate is None else jnp.where(gate(chip), 1.0, 0.0)
            parts.append(decoder(ref.at[g], k, factor))
        sums = []
        for i in range(GROUP):
            tile = acc[base + g * GROUP + i]
            for part in parts:
                tile = tile + part(i)
            if form == "message":
                sums.append(tile)
            elif form == "tiles":
                result[g * GROUP + i] = tile.astype(result.dtype)
            else:
                out[g, :, i * order : (i + 1) * order] = tile
        if form == "message":
            encode(sums, result.at[g])
        elif form == "rows":
            out_copy(g).start()
    if form == "rows":
        for g in range(groups):
            out_copy(g).wait()


def combine(half, which, acc, sib, arrived, gates, form, into=None):
    chips, groups, rows, order = sib.shape
    k = acc.shape[1]
    operands = [near(x) for x in (acc, sib, *arrived)]
    specs = [NEAR] * len(operands)
    aliases, scratch, out_spec = {}, [], NEAR
    if form == "message":
        out_shape = pltpu.VMEM((groups, rows, order), jnp.int16)
    elif form == "tiles":
        out_shape = pltpu.VMEM((groups * GROUP, k, order), jnp.bfloat16)
    else:
        shard = acc.shape[0] // (2 * chips)
        out_shape = jax.ShapeDtypeStruct((k, shard * order), jnp.float32)
        out_spec = FAR
        scratch = [pltpu.VMEM((groups, k, GROUP * order), jnp.float32), pltpu.SemaphoreType.DMA((groups,))]
        if into is not None:
            aliases = {len(operands): 0}
            operands.append(into)
            specs.append(FAR)
    return pl.pallas_call(
        functools.partial(combine_kernel, half, which, gates, form),
        out_shape=out_shape,
        in_specs=specs,
        out_specs=out_spec,
        input_output_aliases=aliases,
        scratch_shapes=scratch,
        compiler_params=pltpu.CompilerParams(vmem_limit_bytes=SMALL),
        name="combine_" + form,
    )(*operands)


def chip_moves(moves):
    return [(2 * a + core, 2 * b + core) for a, b in moves for core in range(2)]


def is_end(chip):
    return (chip == 0) | (chip == 3)


def is_inner(chip):
    return (chip == 1) | (chip == 2)


END_MOVES = [(0, 1), (3, 2)]
MOVES_A = [(0, 1), (1, 0), (2, 3), (3, 2)]
MOVES_B = END_MOVES + [(1, 3), (2, 0)]
MOVES_D = [(1, 2), (2, 1)]
ARRIVED_GATES = (is_end, is_end, None, None)


def move(x, moves):
    return lax.ppermute(x, "col", chip_moves(moves))


def walk_line(summed, form):
    got_a = move(summed(lambda z: 3 - 3 * (z % 2), (), (), "message"), MOVES_A)
    got_b = move(summed(lambda z: z ^ 2, (got_a,), (is_inner,), "message"), MOVES_B)
    send = summed(lambda z: 1 + z % 2, (got_b,), (is_inner,), "message")
    return summed(lambda z: z, (got_a, got_b, move(send, END_MOVES), move(send, MOVES_D)), ARRIVED_GATES, form)


def swap_cores(msg):
    return lax.ppermute(msg, "col", [(c, c ^ 1) for c in range(2 * msg.shape[0])])


def line_sum(half, acc, msg, form, into=None):
    chips = msg.shape[0]
    sib = swap_cores(msg)

    def summed(which, arrived, gates, form):
        return combine(half, which, acc, sib, arrived, gates, form, into if form == "rows" else None)

    if chips == 4:
        return walk_line(summed, form)
    arrived = ()
    for step in range(1, chips):
        send = summed(lambda z: (z + step) % chips, (), (), "message")
        arrived += (move(send, [(a, (a + step) % chips) for a in range(chips)]),)
    return summed(lambda z: z, arrived, (None,) * len(arrived), form)


def spread_kernel(half, acc, sib, *results):
    groups = sib.shape[1]
    k = acc.shape[1]
    shard = acc.shape[0] // 8
    row_owner, core = lax.axis_index("row"), lax.axis_index("col") % 2
    for flip, result in enumerate(results):
        part = row_owner ^ flip

        @pl.loop(0, groups)
        def _(g):
            base = (core * 4 + part) * shard + (half * groups + g) * GROUP
            other = decoder(sib.at[part, g], k)
            encode([acc[base + i] + other(i) for i in range(GROUP)], result.at[g])


def relay_kernel(which, gates, form, *refs):
    parts, arrived, result = refs[:4], refs[4:-1], refs[-1]
    groups, rows, _ = parts[0].shape
    k = (rows - 16) // GROUP
    chip = lax.axis_index("col") // 2
    wanted = lax.axis_index("row") ^ which(chip)
    for flip, part in enumerate(parts):

        @pl.when(wanted == flip)
        def _():
            if form == "message" and not arrived:
                result[...] = part[...]
                return

            @pl.loop(0, groups)
            def _(g):
                terms = [decoder(part.at[g], k)]
                for ref, gate in zip(arrived, gates):
                    factor = None if gate is None else jnp.where(gate(chip), 1.0, 0.0)
                    terms.append(decoder(ref.at[g], k, factor))
                sums = [functools.reduce(jnp.add, [term(i) for term in terms]) for i in range(GROUP)]
                if form == "message":
                    encode(sums, result.at[g])
                else:
                    for i in range(GROUP):
                        result[g * GROUP + i] = sums[i].astype(result.dtype)


def small_call(kernel, name, out_shape, operands):
    many = isinstance(out_shape, tuple)
    return pl.pallas_call(
        kernel,
        out_shape=out_shape,
        in_specs=[NEAR] * len(operands),
        out_specs=(NEAR,) * len(out_shape) if many else NEAR,
        compiler_params=pltpu.CompilerParams(vmem_limit_bytes=SMALL),
        name=name,
    )(*[near(x) for x in operands])


def plane_sum(half, acc, msg):
    _, groups, rows, order = msg.shape
    message = pltpu.VMEM((groups, rows, order), jnp.int16)
    tiles = pltpu.VMEM((groups * GROUP, acc.shape[1], order), jnp.bfloat16)
    sent = small_call(functools.partial(spread_kernel, half), "spread", (message,) * 4, (acc, swap_cores(msg)))
    parts = sent[:1] + tuple(across(sent[flip], flip) for flip in (1, 2, 3))

    def summed(which, arrived, gates, form):
        kernel = functools.partial(relay_kernel, which, gates, form)
        return small_call(kernel, "relay_" + form, message if form == "message" else tiles, parts + arrived)

    return walk_line(summed, "tiles")


def across(x, flip):
    return lax.ppermute(x, "row", [(r, r ^ flip) for r in range(4)])


def gather_square(low, high):
    y_low = across(low, 2)
    x_high = across(high, 1)
    x_low = across(low, 1)
    y_high = across(high, 2)
    return low, high, x_low, x_high, y_low, y_high, across(y_low, 1), across(x_high, 2)


def gather_panel(low, high, row_total):
    shard = 2 * low.shape[0]
    if row_total != 4:
        tiles = jnp.concatenate([low, high], axis=0)
        return (lax.all_gather(tiles, "row", axis=0, tiled=True),), lambda c, r: c
    return gather_square(low, high), lambda c, r: c ^ (r * shard)


def shards(row_total, col_total, vectors, blocks, block_rows, block_cols, counts):
    k, width = vectors.shape
    order = blocks.shape[2]
    shard = width // order
    square = (row_total, col_total) == (4, 8)
    sizes = (row_total * shard, col_total * shard + 1, k, order)
    index = (block_rows, block_cols, counts, shard, col_total)
    tiles = vectors.reshape(k, shard, order).transpose(1, 0, 2)
    pieces, place = gather_panel(tiles[: shard // 2], tiles[shard // 2 :], row_total)
    early = len(pieces) * 3 // 4
    panel, acc, held = prepare(pieces[:early], *sizes, counts, blocks[0])
    acc, low, high = block_product(pieces[early:], place, square, panel, acc, held, *index)
    if square:
        low, high = plane_sum(0, acc, low), plane_sum(1, acc, high)
    else:
        moves = []
        for s in range(row_total * col_total):
            moves.append((s, (s % row_total) * col_total + s // row_total))
        low, high = line_sum(0, acc, low, "tiles"), line_sum(1, acc, high, "tiles")
        low, high = (lax.ppermute(x, ("row", "col"), moves) for x in (low, high))
    pieces, place = gather_panel(low, high, row_total)
    panel, acc = prepare(pieces[:early], *sizes, counts)
    acc, low, high = block_product(pieces[early:], place, False, panel, acc, held, *index)
    return line_sum(1, acc, high, "rows", line_sum(0, acc, low, "rows"))


def solution(mesh):
    in_specs = (
        P(None, ("col", "row")),
        P("row", "col", None, None),
        P("row", "col"),
        P("row", "col"),
        P("row", "col"),
    )
    out_specs = P(None, ("row", "col"))
    body = functools.partial(shards, mesh.shape["row"], mesh.shape["col"])
    return jax.shard_map(body, mesh=mesh, in_specs=in_specs, out_specs=out_specs, check_vma=False)
```

```python
import functools

import jax
import jax.numpy as jnp
from jax import lax
from jax.experimental import pallas as pl
from jax.experimental.pallas import tpu as pltpu
from jax.sharding import PartitionSpec as P

GROUP = 8
STEP = 64
TOP = 14.0
SMALL = 4 * 1024 * 1024

def message_rows(vec_width):
    return GROUP * vec_width + 16


def encode(tiles, ref):
    k = tiles[0].shape[0]
    exponents = []
    for i, tile in enumerate(tiles):
        peak = jnp.max(jnp.abs(tile), axis=0, keepdims=True)
        exponent = jnp.ceil(jnp.log2(jnp.maximum(peak, 1e-30)))
        scaled = jnp.round(tile * jnp.exp2(TOP - exponent))
        ref[i * k : (i + 1) * k, :] = scaled.astype(jnp.int32).astype(jnp.int16)
        exponents.append(exponent)
    rest = jnp.zeros((16 - len(tiles), tiles[0].shape[1]), jnp.float32)
    table = jnp.concatenate(exponents + [rest], axis=0)
    ref[len(tiles) * k :, :] = table.astype(jnp.int32).astype(jnp.int16)


def decoder(ref, k, factor=None):
    table = ref[GROUP * k :, :].astype(jnp.int32).astype(jnp.float32)
    scale = jnp.exp2(table - TOP)
    if factor is not None:
        scale = scale * factor

    def tile(i):
        codes = ref[i * k : (i + 1) * k, :].astype(jnp.int32).astype(jnp.float32)
        return codes * scale[i : i + 1, :]

    return tile


def near(x):
    return pltpu.with_memory_space_constraint(x, pltpu.VMEM)


NEAR = pl.BlockSpec(memory_space=pltpu.VMEM)
FAR = pl.BlockSpec(memory_space=pltpu.HBM)


def prepare_kernel(load, count, *refs):
    total = len(refs) - (5 if load else 3)
    pieces = refs[:total]
    if load:
        blocks, panel, acc, held, sem = refs[total:]
        slots = blocks.shape[0]
        n = count[0, 0]

        def block_copy(i):
            span = pl.ds(i * STEP, STEP)
            return pltpu.make_async_copy(blocks.at[span], held.at[span], sem.at[i])

        for i in range(slots // STEP):

            @pl.when(i * STEP < n)
            def _():
                block_copy(i).start()
    else:
        panel, acc, sem = refs[total:]

    def piece_copy(i):
        tiles = pieces[i].shape[0]
        return pltpu.make_async_copy(pieces[i], panel.at[pl.ds(i * tiles, tiles)], sem.at[sem.shape[0] - 1 - i])

    for i in range(total):
        piece_copy(i).start()

    @pl.loop(0, acc.shape[0])
    def _(i):
        acc[i] = jnp.zeros_like(acc[0])

    for i in range(total):
        piece_copy(i).wait()
    if load:
        for i in range(slots // STEP):

            @pl.when(i * STEP < n)
            def _():
                block_copy(i).wait()


def prepare(pieces, panel_tiles, acc_tiles, k, order, counts, blocks=None):
    operands = [near(p) for p in pieces]
    specs = [pl.BlockSpec(memory_space=pltpu.SMEM)] + [NEAR] * len(pieces)
    out_shape = [
        pltpu.VMEM((panel_tiles, k, order), jnp.bfloat16),
        pltpu.VMEM((acc_tiles, k, order), jnp.float32),
    ]
    copies = len(pieces)
    if blocks is not None:
        operands.append(pltpu.with_memory_space_constraint(blocks, pltpu.HBM))
        specs.append(FAR)
        out_shape.append(pltpu.VMEM(blocks.shape, blocks.dtype))
        copies += blocks.shape[0] // STEP
    return pl.pallas_call(
        functools.partial(prepare_kernel, blocks is not None),
        out_shape=tuple(out_shape),
        in_specs=specs,
        out_specs=(NEAR,) * len(out_shape),
        scratch_shapes=[pltpu.SemaphoreType.DMA((max(copies, 1),))],
        compiler_params=pltpu.CompilerParams(vmem_limit_bytes=SMALL),
        name="prepare",
    )(counts, *operands)


def product_kernel(place, halves, shard, rows, cols, count, panel_in, acc_in, held, *refs):
    total = len(refs) - 5
    pieces = refs[:total]
    panel, acc, msg_low, msg_high, sem = refs[total:]
    chips, groups = msg_low.shape[:2]
    k = panel.shape[1]
    row_total = acc.shape[0] - 1
    n = count[0, 0]
    row_owner, col_owner = lax.axis_index("row"), lax.axis_index("col")

    def piece_copy(i):
        tiles = pieces[i].shape[0]
        start = panel.shape[0] - (total - i) * tiles
        return pltpu.make_async_copy(pieces[i], panel.at[pl.ds(start, tiles)], sem.at[i])

    for i in range(total):
        piece_copy(i).start()
    for i in range(total):
        piece_copy(i).wait()

    @pl.loop(0, (n + STEP - 1) // STEP)
    def _(step):
        base = step * STEP
        nil = jnp.zeros(panel.shape[1:], panel.dtype)

        def entry(u):
            return panel[place(cols[0, base + u], row_owner)]

        products = []
        for u in range(0, STEP, 2):
            upper = jnp.concatenate([entry(u), nil], axis=1)
            lower = jnp.concatenate([nil, entry(u + 1)], axis=1)
            both = lax.dot_general(
                jnp.concatenate([upper, lower], axis=0),
                jnp.concatenate([held[base + u], held[base + u + 1]], axis=1),
                (((1,), (1,)), ((), ())),
                preferred_element_type=jnp.float32,
            )
            products += [both[:k], both[k:]]
        for u in range(STEP):
            at = jnp.where(base + u < n, rows[0, base + u], row_total)
            acc[at] += products[u]

    other = 1 - col_owner % 2
    for half, msg in enumerate((msg_low, msg_high)):

        @pl.loop(0, chips * groups)
        def _(i):
            d, g = i // groups, i % groups
            owner = other * chips + d if halves else 2 * d + other
            base = owner * shard + (half * groups + g) * GROUP
            encode([acc[base + t] for t in range(GROUP)], msg.at[d, g])


def block_product(late, place, halves, panel, acc, held, block_rows, block_cols, counts, shard, col_total):
    _, k, order = panel.shape
    scalars = pl.BlockSpec(memory_space=pltpu.SMEM)
    message = pltpu.VMEM((col_total // 2, shard // GROUP // 2, message_rows(k), order), jnp.int16)
    return pl.pallas_call(
        functools.partial(product_kernel, place, halves, shard),
        out_shape=(pltpu.VMEM(panel.shape, panel.dtype), pltpu.VMEM(acc.shape, acc.dtype), message, message),
        in_specs=[scalars] * 3 + [NEAR] * (3 + len(late)),
        out_specs=(NEAR,) * 4,
        input_output_aliases={3: 0, 4: 1},
        scratch_shapes=[pltpu.SemaphoreType.DMA((max(len(late), 1),))],
        compiler_params=pltpu.CompilerParams(vmem_limit_bytes=SMALL),
        name="block_product",
    )(block_rows, block_cols, counts, near(panel), near(acc), near(held), *[near(p) for p in late])[1:]


def combine_kernel(half, which, gates, form, acc, sib, *refs):
    arrived = refs[: len(gates)]
    chips, groups = sib.shape[:2]
    _, k, order = acc.shape
    shard = acc.shape[0] // (2 * chips)
    col_owner = lax.axis_index("col")
    chip = col_owner // 2
    d = which(chip)
    base = (2 * d + col_owner % 2) * shard + half * groups * GROUP
    if form == "rows":
        result, out, out_sem = refs[-3:]
    else:
        result = refs[-1]

    def out_copy(g):
        width = GROUP * order
        there = result.at[:, pl.ds((half * groups + g) * width, width)]
        return pltpu.make_async_copy(out.at[g], there, out_sem.at[g])

    for g in range(groups):
        parts = [decoder(sib.at[d, g], k)]
        for ref, gate in zip(arrived, gates):
            factor = None if gate is None else jnp.where(gate(chip), 1.0, 0.0)
            parts.append(decoder(ref.at[g], k, factor))
        sums = []
        for i in range(GROUP):
            tile = acc[base + g * GROUP + i]
            for part in parts:
                tile = tile + part(i)
            if form == "message":
                sums.append(tile)
            elif form == "tiles":
                result[g * GROUP + i] = tile.astype(result.dtype)
            else:
                out[g, :, i * order : (i + 1) * order] = tile
        if form == "message":
            encode(sums, result.at[g])
        elif form == "rows":
            out_copy(g).start()
    if form == "rows":
        for g in range(groups):
            out_copy(g).wait()


def combine(half, which, acc, sib, arrived, gates, form, into=None):
    chips, groups, rows, order = sib.shape
    k = acc.shape[1]
    operands = [near(x) for x in (acc, sib, *arrived)]
    specs = [NEAR] * len(operands)
    aliases, scratch, out_spec = {}, [], NEAR
    if form == "message":
        out_shape = pltpu.VMEM((groups, rows, order), jnp.int16)
    elif form == "tiles":
        out_shape = pltpu.VMEM((groups * GROUP, k, order), jnp.bfloat16)
    else:
        shard = acc.shape[0] // (2 * chips)
        out_shape = jax.ShapeDtypeStruct((k, shard * order), jnp.float32)
        out_spec = FAR
        scratch = [pltpu.VMEM((groups, k, GROUP * order), jnp.float32), pltpu.SemaphoreType.DMA((groups,))]
        if into is not None:
            aliases = {len(operands): 0}
            operands.append(into)
            specs.append(FAR)
    return pl.pallas_call(
        functools.partial(combine_kernel, half, which, gates, form),
        out_shape=out_shape,
        in_specs=specs,
        out_specs=out_spec,
        input_output_aliases=aliases,
        scratch_shapes=scratch,
        compiler_params=pltpu.CompilerParams(vmem_limit_bytes=SMALL),
        name="combine_" + form,
    )(*operands)


def chip_moves(moves):
    return [(2 * a + core, 2 * b + core) for a, b in moves for core in range(2)]


def is_end(chip):
    return (chip == 0) | (chip == 3)


def is_inner(chip):
    return (chip == 1) | (chip == 2)


END_MOVES = [(0, 1), (3, 2)]
MOVES_A = [(0, 1), (1, 0), (2, 3), (3, 2)]
MOVES_B = END_MOVES + [(1, 3), (2, 0)]
MOVES_D = [(1, 2), (2, 1)]
ARRIVED_GATES = (is_end, is_end, None, None)


def move(x, moves):
    return lax.ppermute(x, "col", chip_moves(moves))


def walk_line(summed, form):
    got_a = move(summed(lambda z: 3 - 3 * (z % 2), (), (), "message"), MOVES_A)
    got_b = move(summed(lambda z: z ^ 2, (got_a,), (is_inner,), "message"), MOVES_B)
    send = summed(lambda z: 1 + z % 2, (got_b,), (is_inner,), "message")
    return summed(lambda z: z, (got_a, got_b, move(send, END_MOVES), move(send, MOVES_D)), ARRIVED_GATES, form)


def swap_cores(msg):
    return lax.ppermute(msg, "col", [(c, c ^ 1) for c in range(2 * msg.shape[0])])


def line_sum(half, acc, msg, form, into=None):
    chips = msg.shape[0]
    sib = swap_cores(msg)

    def summed(which, arrived, gates, form):
        return combine(half, which, acc, sib, arrived, gates, form, into if form == "rows" else None)

    if chips == 4:
        return walk_line(summed, form)
    arrived = ()
    for step in range(1, chips):
        send = summed(lambda z: (z + step) % chips, (), (), "message")
        arrived += (move(send, [(a, (a + step) % chips) for a in range(chips)]),)
    return summed(lambda z: z, arrived, (None,) * len(arrived), form)


def spread_kernel(half, acc, sib, *results):
    groups = sib.shape[1]
    k = acc.shape[1]
    shard = acc.shape[0] // 8
    row_owner, core = lax.axis_index("row"), lax.axis_index("col") % 2
    for flip, result in enumerate(results):
        part = row_owner ^ flip

        @pl.loop(0, groups)
        def _(g):
            base = (core * 4 + part) * shard + (half * groups + g) * GROUP
            other = decoder(sib.at[part, g], k)
            encode([acc[base + i] + other(i) for i in range(GROUP)], result.at[g])


def relay_kernel(which, gates, form, *refs):
    parts, arrived, result = refs[:4], refs[4:-1], refs[-1]
    groups, rows, _ = parts[0].shape
    k = (rows - 16) // GROUP
    chip = lax.axis_index("col") // 2
    wanted = lax.axis_index("row") ^ which(chip)
    for flip, part in enumerate(parts):

        @pl.when(wanted == flip)
        def _():
            if form == "message" and not arrived:
                result[...] = part[...]
                return

            @pl.loop(0, groups)
            def _(g):
                terms = [decoder(part.at[g], k)]
                for ref, gate in zip(arrived, gates):
                    factor = None if gate is None else jnp.where(gate(chip), 1.0, 0.0)
                    terms.append(decoder(ref.at[g], k, factor))
                sums = [functools.reduce(jnp.add, [term(i) for term in terms]) for i in range(GROUP)]
                if form == "message":
                    encode(sums, result.at[g])
                else:
                    for i in range(GROUP):
                        result[g * GROUP + i] = sums[i].astype(result.dtype)


def small_call(kernel, name, out_shape, operands):
    many = isinstance(out_shape, tuple)
    return pl.pallas_call(
        kernel,
        out_shape=out_shape,
        in_specs=[NEAR] * len(operands),
        out_specs=(NEAR,) * len(out_shape) if many else NEAR,
        compiler_params=pltpu.CompilerParams(vmem_limit_bytes=SMALL),
        name=name,
    )(*[near(x) for x in operands])


def plane_sum(half, acc, msg):
    _, groups, rows, order = msg.shape
    message = pltpu.VMEM((groups, rows, order), jnp.int16)
    tiles = pltpu.VMEM((groups * GROUP, acc.shape[1], order), jnp.bfloat16)
    sent = small_call(functools.partial(spread_kernel, half), "spread", (message,) * 4, (acc, swap_cores(msg)))
    parts = sent[:1] + tuple(across(sent[flip], flip) for flip in (1, 2, 3))

    def summed(which, arrived, gates, form):
        kernel = functools.partial(relay_kernel, which, gates, form)
        return small_call(kernel, "relay_" + form, message if form == "message" else tiles, parts + arrived)

    return walk_line(summed, "tiles")


def across(x, flip):
    return lax.ppermute(x, "row", [(r, r ^ flip) for r in range(4)])


def gather_square(low, high):
    y_low = across(low, 2)
    x_high = across(high, 1)
    x_low = across(low, 1)
    y_high = across(high, 2)
    return low, high, x_low, x_high, y_low, y_high, across(y_low, 1), across(x_high, 2)


def gather_panel(low, high, row_total):
    shard = 2 * low.shape[0]
    if row_total != 4:
        tiles = jnp.concatenate([low, high], axis=0)
        return (lax.all_gather(tiles, "row", axis=0, tiled=True),), lambda c, r: c
    return gather_square(low, high), lambda c, r: c ^ (r * shard)


def shards(row_total, col_total, vectors, blocks, block_rows, block_cols, counts):
    k, width = vectors.shape
    order = blocks.shape[2]
    shard = width // order
    square = (row_total, col_total) == (4, 8)
    sizes = (row_total * shard, col_total * shard + 1, k, order)
    index = (block_rows, block_cols, counts, shard, col_total)
    tiles = vectors.reshape(k, shard, order).transpose(1, 0, 2)
    pieces, place = gather_panel(tiles[: shard // 2], tiles[shard // 2 :], row_total)
    early = len(pieces) * 3 // 4
    panel, acc, held = prepare(pieces[:early], *sizes, counts, blocks[0])
    acc, low, high = block_product(pieces[early:], place, square, panel, acc, held, *index)
    if square:
        low, high = plane_sum(0, acc, low), plane_sum(1, acc, high)
    else:
        moves = []
        for s in range(row_total * col_total):
            moves.append((s, (s % row_total) * col_total + s // row_total))
        low, high = line_sum(0, acc, low, "tiles"), line_sum(1, acc, high, "tiles")
        low, high = (lax.ppermute(x, ("row", "col"), moves) for x in (low, high))
    pieces, place = gather_panel(low, high, row_total)
    panel, acc = prepare(pieces[:early], *sizes, counts)
    acc, low, high = block_product(pieces[early:], place, False, panel, acc, held, *index)
    return line_sum(1, acc, high, "rows", line_sum(0, acc, low, "rows"))


def solution(mesh):
    in_specs = (
        P(None, ("col", "row")),
        P("row", "col", None, None),
        P("row", "col"),
        P("row", "col"),
        P("row", "col"),
    )
    out_specs = P(None, ("row", "col"))
    body = functools.partial(shards, mesh.shape["row"], mesh.shape["col"])
    return jax.shard_map(body, mesh=mesh, in_specs=in_specs, out_specs=out_specs, check_vma=False)
```

```python
import functools

import jax
import jax.numpy as jnp
from jax import lax
from jax.experimental import pallas as pl
from jax.experimental.pallas import tpu as pltpu
from jax.sharding import PartitionSpec as P

GROUP = 8
STEP = 64
TOP = 14.0
SMALL = 4 * 1024 * 1024

def message_rows(vec_width):
    return GROUP * vec_width + 16


def encode(tiles, ref):
    k = tiles[0].shape[0]
    exponents = []
    for i, tile in enumerate(tiles):
        peak = jnp.max(jnp.abs(tile), axis=0, keepdims=True)
        exponent = jnp.ceil(jnp.log2(jnp.maximum(peak, 1e-30)))
        scaled = jnp.round(tile * jnp.exp2(TOP - exponent))
        ref[i * k : (i + 1) * k, :] = scaled.astype(jnp.int32).astype(jnp.int16)
        exponents.append(exponent)
    rest = jnp.zeros((16 - len(tiles), tiles[0].shape[1]), jnp.float32)
    table = jnp.concatenate(exponents + [rest], axis=0)
    ref[len(tiles) * k :, :] = table.astype(jnp.int32).astype(jnp.int16)


def decoder(ref, k, factor=None):
    table = ref[GROUP * k :, :].astype(jnp.int32).astype(jnp.float32)
    scale = jnp.exp2(table - TOP)
    if factor is not None:
        scale = scale * factor

    def tile(i):
        codes = ref[i * k : (i + 1) * k, :].astype(jnp.int32).astype(jnp.float32)
        return codes * scale[i : i + 1, :]

    return tile


def near(x):
    return pltpu.with_memory_space_constraint(x, pltpu.VMEM)


NEAR = pl.BlockSpec(memory_space=pltpu.VMEM)
FAR = pl.BlockSpec(memory_space=pltpu.HBM)


def prepare_kernel(load, count, *refs):
    total = len(refs) - (5 if load else 3)
    pieces = refs[:total]
    if load:
        blocks, panel, acc, held, sem = refs[total:]
        slots = blocks.shape[0]
        n = count[0, 0]

        def block_copy(i):
            span = pl.ds(i * STEP, STEP)
            return pltpu.make_async_copy(blocks.at[span], held.at[span], sem.at[i])

        for i in range(slots // STEP):

            @pl.when(i * STEP < n)
            def _():
                block_copy(i).start()
    else:
        panel, acc, sem = refs[total:]

    def piece_copy(i):
        tiles = pieces[i].shape[0]
        return pltpu.make_async_copy(pieces[i], panel.at[pl.ds(i * tiles, tiles)], sem.at[sem.shape[0] - 1 - i])

    for i in range(total):
        piece_copy(i).start()

    @pl.loop(0, acc.shape[0])
    def _(i):
        acc[i] = jnp.zeros_like(acc[0])

    for i in range(total):
        piece_copy(i).wait()
    if load:
        for i in range(slots // STEP):

            @pl.when(i * STEP < n)
            def _():
                block_copy(i).wait()


def prepare(pieces, panel_tiles, acc_tiles, k, order, counts, blocks=None):
    operands = [near(p) for p in pieces]
    specs = [pl.BlockSpec(memory_space=pltpu.SMEM)] + [NEAR] * len(pieces)
    out_shape = [
        pltpu.VMEM((panel_tiles, k, order), jnp.bfloat16),
        pltpu.VMEM((acc_tiles, k, order), jnp.float32),
    ]
    copies = len(pieces)
    if blocks is not None:
        operands.append(pltpu.with_memory_space_constraint(blocks, pltpu.HBM))
        specs.append(FAR)
        out_shape.append(pltpu.VMEM(blocks.shape, blocks.dtype))
        copies += blocks.shape[0] // STEP
    return pl.pallas_call(
        functools.partial(prepare_kernel, blocks is not None),
        out_shape=tuple(out_shape),
        in_specs=specs,
        out_specs=(NEAR,) * len(out_shape),
        scratch_shapes=[pltpu.SemaphoreType.DMA((max(copies, 1),))],
        compiler_params=pltpu.CompilerParams(vmem_limit_bytes=SMALL),
        name="prepare",
    )(counts, *operands)


def product_kernel(place, halves, shard, rows, cols, count, panel_in, acc_in, held, *refs):
    total = len(refs) - 4
    pieces = refs[:total]
    panel, acc, msg_low, sem = refs[total:]
    k = panel.shape[1]
    row_total = acc.shape[0] - 1
    n = count[0, 0]
    row_owner, col_owner = lax.axis_index("row"), lax.axis_index("col")

    def piece_copy(i):
        tiles = pieces[i].shape[0]
        start = panel.shape[0] - (total - i) * tiles
        return pltpu.make_async_copy(pieces[i], panel.at[pl.ds(start, tiles)], sem.at[i])

    for i in range(total):
        piece_copy(i).start()
    for i in range(total):
        piece_copy(i).wait()

    @pl.loop(0, (n + STEP - 1) // STEP)
    def _(step):
        base = step * STEP
        nil = jnp.zeros(panel.shape[1:], panel.dtype)

        def entry(u):
            return panel[place(cols[0, base + u], row_owner)]

        products = []
        for u in range(0, STEP, 2):
            upper = jnp.concatenate([entry(u), nil], axis=1)
            lower = jnp.concatenate([nil, entry(u + 1)], axis=1)
            both = lax.dot_general(
                jnp.concatenate([upper, lower], axis=0),
                jnp.concatenate([held[base + u], held[base + u + 1]], axis=1),
                (((1,), (1,)), ((), ())),
                preferred_element_type=jnp.float32,
            )
            products += [both[:k], both[k:]]
        for u in range(STEP):
            at = jnp.where(base + u < n, rows[0, base + u], row_total)
            acc[at] += products[u]

    encode_half(0, halves, shard, acc, msg_low)


def encode_half(half, halves, shard, acc, msg):
    chips, groups = msg.shape[:2]
    other = 1 - lax.axis_index("col") % 2

    @pl.loop(0, chips * groups)
    def _(i):
        d, g = i // groups, i % groups
        owner = other * chips + d if halves else 2 * d + other
        base = owner * shard + (half * groups + g) * GROUP
        encode([acc[base + t] for t in range(GROUP)], msg.at[d, g])


def block_product(late, place, halves, panel, acc, held, block_rows, block_cols, counts, shard, col_total):
    _, k, order = panel.shape
    scalars = pl.BlockSpec(memory_space=pltpu.SMEM)
    message = pltpu.VMEM((col_total // 2, shard // GROUP // 2, message_rows(k), order), jnp.int16)
    _, acc, low = pl.pallas_call(
        functools.partial(product_kernel, place, halves, shard),
        out_shape=(pltpu.VMEM(panel.shape, panel.dtype), pltpu.VMEM(acc.shape, acc.dtype), message),
        in_specs=[scalars] * 3 + [NEAR] * (3 + len(late)),
        out_specs=(NEAR,) * 3,
        input_output_aliases={3: 0, 4: 1},
        scratch_shapes=[pltpu.SemaphoreType.DMA((max(len(late), 1),))],
        compiler_params=pltpu.CompilerParams(vmem_limit_bytes=SMALL),
        name="block_product",
    )(block_rows, block_cols, counts, near(panel), near(acc), near(held), *[near(p) for p in late])
    return acc, low, small_call(functools.partial(encode_half, 1, halves, shard), "encode_half", message, (acc,))


def combine_kernel(half, which, gates, form, acc, sib, *refs):
    arrived = refs[: len(gates)]
    chips, groups = sib.shape[:2]
    _, k, order = acc.shape
    shard = acc.shape[0] // (2 * chips)
    col_owner = lax.axis_index("col")
    chip = col_owner // 2
    d = which(chip)
    base = (2 * d + col_owner % 2) * shard + half * groups * GROUP
    if form == "rows":
        result, out, out_sem = refs[-3:]
    else:
        result = refs[-1]

    def out_copy(g):
        width = GROUP * order
        there = result.at[:, pl.ds((half * groups + g) * width, width)]
        return pltpu.make_async_copy(out.at[g], there, out_sem.at[g])

    for g in range(groups):
        parts = [decoder(sib.at[d, g], k)]
        for ref, gate in zip(arrived, gates):
            factor = None if gate is None else jnp.where(gate(chip), 1.0, 0.0)
            parts.append(decoder(ref.at[g], k, factor))
        sums = []
        for i in range(GROUP):
            tile = acc[base + g * GROUP + i]
            for part in parts:
                tile = tile + part(i)
            if form == "message":
                sums.append(tile)
            elif form == "tiles":
                result[g * GROUP + i] = tile.astype(result.dtype)
            else:
                out[g, :, i * order : (i + 1) * order] = tile
        if form == "message":
            encode(sums, result.at[g])
        elif form == "rows":
            out_copy(g).start()
    if form == "rows":
        for g in range(groups):
            out_copy(g).wait()


def combine(half, which, acc, sib, arrived, gates, form, into=None):
    chips, groups, rows, order = sib.shape
    k = acc.shape[1]
    operands = [near(x) for x in (acc, sib, *arrived)]
    specs = [NEAR] * len(operands)
    aliases, scratch, out_spec = {}, [], NEAR
    if form == "message":
        out_shape = pltpu.VMEM((groups, rows, order), jnp.int16)
    elif form == "tiles":
        out_shape = pltpu.VMEM((groups * GROUP, k, order), jnp.bfloat16)
    else:
        shard = acc.shape[0] // (2 * chips)
        out_shape = jax.ShapeDtypeStruct((k, shard * order), jnp.float32)
        out_spec = FAR
        scratch = [pltpu.VMEM((groups, k, GROUP * order), jnp.float32), pltpu.SemaphoreType.DMA((groups,))]
        if into is not None:
            aliases = {len(operands): 0}
            operands.append(into)
            specs.append(FAR)
    return pl.pallas_call(
        functools.partial(combine_kernel, half, which, gates, form),
        out_shape=out_shape,
        in_specs=specs,
        out_specs=out_spec,
        input_output_aliases=aliases,
        scratch_shapes=scratch,
        compiler_params=pltpu.CompilerParams(vmem_limit_bytes=SMALL),
        name="combine_" + form,
    )(*operands)


def chip_moves(moves):
    return [(2 * a + core, 2 * b + core) for a, b in moves for core in range(2)]


def is_end(chip):
    return (chip == 0) | (chip == 3)


def is_inner(chip):
    return (chip == 1) | (chip == 2)


END_MOVES = [(0, 1), (3, 2)]
MOVES_A = [(0, 1), (1, 0), (2, 3), (3, 2)]
MOVES_B = END_MOVES + [(1, 3), (2, 0)]
MOVES_D = [(1, 2), (2, 1)]
ARRIVED_GATES = (is_end, is_end, None, None)


def move(x, moves):
    return lax.ppermute(x, "col", chip_moves(moves))


def walk_line(summed, form):
    got_a = move(summed(lambda z: 3 - 3 * (z % 2), (), (), "message"), MOVES_A)
    got_b = move(summed(lambda z: z ^ 2, (got_a,), (is_inner,), "message"), MOVES_B)
    send = summed(lambda z: 1 + z % 2, (got_b,), (is_inner,), "message")
    return summed(lambda z: z, (got_a, got_b, move(send, END_MOVES), move(send, MOVES_D)), ARRIVED_GATES, form)


def swap_cores(msg):
    return lax.ppermute(msg, "col", [(c, c ^ 1) for c in range(2 * msg.shape[0])])


def line_sum(half, acc, msg, form, into=None):
    chips = msg.shape[0]
    sib = swap_cores(msg)

    def summed(which, arrived, gates, form):
        return combine(half, which, acc, sib, arrived, gates, form, into if form == "rows" else None)

    if chips == 4:
        return walk_line(summed, form)
    arrived = ()
    for step in range(1, chips):
        send = summed(lambda z: (z + step) % chips, (), (), "message")
        arrived += (move(send, [(a, (a + step) % chips) for a in range(chips)]),)
    return summed(lambda z: z, arrived, (None,) * len(arrived), form)


def spread_kernel(half, acc, sib, *results):
    groups = sib.shape[1]
    k = acc.shape[1]
    shard = acc.shape[0] // 8
    row_owner, core = lax.axis_index("row"), lax.axis_index("col") % 2
    for flip, result in enumerate(results):
        part = row_owner ^ flip

        @pl.loop(0, groups)
        def _(g):
            base = (core * 4 + part) * shard + (half * groups + g) * GROUP
            other = decoder(sib.at[part, g], k)
            encode([acc[base + i] + other(i) for i in range(GROUP)], result.at[g])


def relay_kernel(which, gates, form, *refs):
    parts, arrived, result = refs[:4], refs[4:-1], refs[-1]
    groups, rows, _ = parts[0].shape
    k = (rows - 16) // GROUP
    chip = lax.axis_index("col") // 2
    wanted = lax.axis_index("row") ^ which(chip)
    for flip, part in enumerate(parts):

        @pl.when(wanted == flip)
        def _():
            if form == "message" and not arrived:
                result[...] = part[...]
                return

            @pl.loop(0, groups)
            def _(g):
                terms = [decoder(part.at[g], k)]
                for ref, gate in zip(arrived, gates):
                    factor = None if gate is None else jnp.where(gate(chip), 1.0, 0.0)
                    terms.append(decoder(ref.at[g], k, factor))
                sums = [functools.reduce(jnp.add, [term(i) for term in terms]) for i in range(GROUP)]
                if form == "message":
                    encode(sums, result.at[g])
                else:
                    for i in range(GROUP):
                        result[g * GROUP + i] = sums[i].astype(result.dtype)


def small_call(kernel, name, out_shape, operands):
    many = isinstance(out_shape, tuple)
    return pl.pallas_call(
        kernel,
        out_shape=out_shape,
        in_specs=[NEAR] * len(operands),
        out_specs=(NEAR,) * len(out_shape) if many else NEAR,
        compiler_params=pltpu.CompilerParams(vmem_limit_bytes=SMALL),
        name=name,
    )(*[near(x) for x in operands])


def plane_sum(half, acc, msg):
    _, groups, rows, order = msg.shape
    message = pltpu.VMEM((groups, rows, order), jnp.int16)
    tiles = pltpu.VMEM((groups * GROUP, acc.shape[1], order), jnp.bfloat16)
    sent = small_call(functools.partial(spread_kernel, half), "spread", (message,) * 4, (acc, swap_cores(msg)))
    parts = sent[:1] + tuple(across(sent[flip], flip) for flip in (1, 2, 3))

    def summed(which, arrived, gates, form):
        kernel = functools.partial(relay_kernel, which, gates, form)
        return small_call(kernel, "relay_" + form, message if form == "message" else tiles, parts + arrived)

    return walk_line(summed, "tiles")


def across(x, flip):
    return lax.ppermute(x, "row", [(r, r ^ flip) for r in range(4)])


def gather_square(low, high):
    y_low = across(low, 2)
    x_high = across(high, 1)
    x_low = across(low, 1)
    y_high = across(high, 2)
    return low, high, x_low, x_high, y_low, y_high, across(y_low, 1), across(x_high, 2)


def gather_panel(low, high, row_total):
    shard = 2 * low.shape[0]
    if row_total != 4:
        tiles = jnp.concatenate([low, high], axis=0)
        return (lax.all_gather(tiles, "row", axis=0, tiled=True),), lambda c, r: c
    return gather_square(low, high), lambda c, r: c ^ (r * shard)


def shards(row_total, col_total, vectors, blocks, block_rows, block_cols, counts):
    k, width = vectors.shape
    order = blocks.shape[2]
    shard = width // order
    square = (row_total, col_total) == (4, 8)
    sizes = (row_total * shard, col_total * shard + 1, k, order)
    index = (block_rows, block_cols, counts, shard, col_total)
    tiles = vectors.reshape(k, shard, order).transpose(1, 0, 2)
    pieces, place = gather_panel(tiles[: shard // 2], tiles[shard // 2 :], row_total)
    early = len(pieces) * 3 // 4
    panel, acc, held = prepare(pieces[:early], *sizes, counts, blocks[0])
    acc, low, high = block_product(pieces[early:], place, square, panel, acc, held, *index)
    if square:
        low, high = plane_sum(0, acc, low), plane_sum(1, acc, high)
    else:
        moves = []
        for s in range(row_total * col_total):
            moves.append((s, (s % row_total) * col_total + s // row_total))
        low, high = line_sum(0, acc, low, "tiles"), line_sum(1, acc, high, "tiles")
        low, high = (lax.ppermute(x, ("row", "col"), moves) for x in (low, high))
    pieces, place = gather_panel(low, high, row_total)
    panel, acc = prepare(pieces[:early], *sizes, counts)
    acc, low, high = block_product(pieces[early:], place, False, panel, acc, held, *index)
    return line_sum(1, acc, high, "rows", line_sum(0, acc, low, "rows"))


def solution(mesh):
    in_specs = (
        P(None, ("col", "row")),
        P("row", "col", None, None),
        P("row", "col"),
        P("row", "col"),
        P("row", "col"),
    )
    out_specs = P(None, ("row", "col"))
    body = functools.partial(shards, mesh.shape["row"], mesh.shape["col"])
    return jax.shard_map(body, mesh=mesh, in_specs=in_specs, out_specs=out_specs, check_vma=False)
```
